128 devices in a mesh: grp: 4 (over x), row: 32 (over z, y, core).
Axes of the slice: x: 4, y: 4, z: 4, core: 2. Of those that a mesh axis runs over, the one named last changes fastest.
Arguments:
- snapshots: bfloat16 [8192, 131072], P(None, ('grp', 'row')), may hold values from -8 to 8
- weights: float32 [131072], P(('grp', 'row')), may hold values from 0.25 to 4
- reference_field: float32 [131072], P(('grp', 'row')), may hold values from -6 to 6
- start_basis: float32 [64, 2, 63, 8], replicated, may hold values from -6 to 6
Outputs:
- spod_modes: float32 [64, 16, 131072], P(None, None, ('grp', 'row'))
- energies: float32 [64, 8], replicated
The draws below stay inside these ranges and needn't reach their ends.
All inputs are finite; a program needn't handle non-finite values.
Results may differ from the reference program's by a relative error of at most 0.012.
The reference program's roundings to bfloat16 on the way count: a program that leaves them out, or rounds other values in their place, can miss the bound.
Values may be sent and summed in bfloat16 or wider, within the bound.
A program may use at most 192 MiB of HBM per device.

```python
import math
import jax
import jax.numpy as jnp
from jax import lax

NFFT = 256
NBLK = 63
NF = 64
NM = 8
ITERS = 12
ROW_DEV = 1024
NT = 8192
NROWS = 131072


def draw_snapshots(key, part):
    shape_count = 32
    key_time, key_shape, key_noise = jax.random.split(jax.random.fold_in(key, 7), 3)
    energy_levels = jnp.sqrt(0.15 * 0.85 ** jnp.arange(shape_count, dtype=jnp.float32))
    position = jnp.arange(NROWS, dtype=jnp.float32) / NROWS
    envelope = 0.6 + 1.2 * position
    temporal = jax.random.normal(key_time, (NT, shape_count), jnp.float32) * energy_levels
    spatial = jax.random.normal(key_shape, (shape_count, NROWS), jnp.float32)
    noise = 0.6 * jax.random.normal(key_noise, (NT, NROWS), jnp.float32)
    field = jnp.dot(temporal, spatial * envelope) + noise
    return jnp.clip(field, -8.0, 8.0).astype(jnp.bfloat16)


def block_levels(stream_key, shape, shards, low, top_value):
    def one(dim, parts):
        steps = jax.random.uniform(jax.random.fold_in(jax.random.fold_in(stream_key, 6), dim), (parts,), jnp.float32, low / len(shards), top_value / len(shards))
        return jnp.repeat(jnp.exp(steps), shape[dim] // parts).reshape((-1,) + (1,) * (len(shape) - dim - 1))

    loudness = one(*shards[0])
    for cut in shards[1:]:
        loudness = loudness * one(*cut)
    return loudness


def bell_draw(key, extent, spread, reach, pieces=(), kind=jnp.bfloat16):
    drawn = spread * jax.random.normal(key, extent, jnp.float32)
    if pieces:
        drawn = drawn * block_levels(key, extent, pieces, -0.22, 0.18)
    return jnp.clip(drawn, -reach, reach).astype(kind)


def setup_inputs(seed: int = 0) -> dict:
    key_list = jax.random.split(jax.random.key(seed), 5)
    snapshots = draw_snapshots(jax.random.fold_in(key_list[4], 71), 0)
    weights = jnp.clip(jnp.exp(math.log(4.0) - 2.7725887 * jax.random.uniform(key_list[1], (NROWS,), jnp.float32) ** block_levels(key_list[1], (NROWS,), ((0, 128),), -0.2, 0.2)), 0.25, 4.0)
    reference_field = bell_draw(key_list[2], (NROWS,), 1.0, 6.0, ((0, 128),), jnp.float32)
    start_basis = bell_draw(key_list[3], (NF, 2, NBLK, NM), 1.0, 6.0, (), jnp.float32)
    return dict(snapshots=snapshots, weights=weights, reference_field=reference_field, start_basis=start_basis)


highest = lax.Precision.HIGHEST

def dft_table():
    time_steps = jnp.arange(NFFT, dtype=jnp.int32)
    freq_bins = jnp.arange(1, NF + 1, dtype=jnp.int32)
    wrapped = freq_bins[:, None] * time_steps[None, :] % NFFT
    angles = 2.0 * math.pi / NFFT * wrapped.astype(jnp.float32)
    window_taper = 0.5 - 0.5 * jnp.cos(2.0 * math.pi / NFFT * time_steps.astype(jnp.float32))
    scaled_taper = window_taper / jnp.sqrt(jnp.sum(window_taper * window_taper))
    stacked = jnp.stack([jnp.cos(angles), -jnp.sin(angles)]) * scaled_taper[None, None, :]
    return stacked.astype(jnp.bfloat16)

def transform(rows_block, root_weight, dft_rows):
    half_len = NFFT // 2
    hop_rows = rows_block.reshape(NBLK + 1, half_len, rows_block.shape[1]).astype(jnp.float32)
    table_wide = dft_rows.astype(jnp.float32)
    leading = jnp.einsum('pft,htx->fphx', table_wide[:, :, :half_len], hop_rows[:NBLK], precision=highest)
    trailing = jnp.einsum('pft,htx->fphx', table_wide[:, :, half_len:], hop_rows[1:], precision=highest)
    return ((leading + trailing) * root_weight).astype(jnp.bfloat16)

def apply_gram(gram_real, gram_imag, basis_real, basis_imag):
    image_real = jnp.einsum('fbc,fck->fbk', gram_real, basis_real, precision=highest) - jnp.einsum('fbc,fck->fbk', gram_imag, basis_imag, precision=highest)
    image_imag = jnp.einsum('fbc,fck->fbk', gram_real, basis_imag, precision=highest) + jnp.einsum('fbc,fck->fbk', gram_imag, basis_real, precision=highest)
    return (image_real, image_imag)

def orthonormalize(image_real, image_imag):
    cols_real = []
    cols_imag = []
    for column in range(image_real.shape[2]):
        target_real = image_real[:, :, column]
        target_imag = image_imag[:, :, column]
        for earlier in range(column):
            prior_real = cols_real[earlier]
            prior_imag = cols_imag[earlier]
            inner_real = lax.optimization_barrier(jnp.sum(prior_real * target_real + prior_imag * target_imag, axis=1, keepdims=True))
            inner_imag = lax.optimization_barrier(jnp.sum(prior_real * target_imag - prior_imag * target_real, axis=1, keepdims=True))
            target_real, target_imag = (target_real - (inner_real * prior_real - inner_imag * prior_imag), target_imag - (inner_real * prior_imag + inner_imag * prior_real))
        length = jnp.sqrt(lax.optimization_barrier(jnp.sum(target_real * target_real + target_imag * target_imag, axis=1, keepdims=True)) + 1e-06)
        cols_real.append(target_real / length)
        cols_imag.append(target_imag / length)
    return (jnp.stack(cols_real, axis=2), jnp.stack(cols_imag, axis=2))

def subspace_solve(gram_real, gram_imag, start_basis):

    def sweep_once(sweep_index, current):
        image_real, image_imag = apply_gram(gram_real, gram_imag, current[0], current[1])
        return orthonormalize(image_real, image_imag)
    basis_real, basis_imag = lax.fori_loop(0, ITERS, sweep_once, (start_basis[:, 0], start_basis[:, 1]))
    image_real, image_imag = apply_gram(gram_real, gram_imag, basis_real, basis_imag)
    energy = lax.optimization_barrier(jnp.sum(basis_real * image_real + basis_imag * image_imag, axis=1))
    return (basis_real, basis_imag, energy)

def coefficient_matrix(basis_real, basis_imag):
    round_real = basis_real.astype(jnp.bfloat16)
    round_imag = basis_imag.astype(jnp.bfloat16)
    upper_half = jnp.concatenate([round_real, round_imag], axis=2)
    lower_half = jnp.concatenate([-round_imag, round_real], axis=2)
    return jnp.stack([upper_half, lower_half], axis=1)

def phase_turn(correlation, energy):
    gain_scale = 1.0 / jnp.sqrt(energy + 1e-06)
    tilt_real = gain_scale * correlation[:, :NM]
    tilt_imag = gain_scale * correlation[:, NM:]
    tilt_size = jnp.sqrt(jnp.maximum(tilt_real * tilt_real + tilt_imag * tilt_imag, 0.25))
    return (gain_scale * tilt_real / tilt_size, -gain_scale * tilt_imag / tilt_size)

def finish(projected, factor_real, factor_imag, root_weight):
    part_real = projected[:, :NM]
    part_imag = projected[:, NM:]
    inverse_root = 1.0 / root_weight
    out_real = (part_real * factor_real[:, :, None] - part_imag * factor_imag[:, :, None]) * inverse_root
    out_imag = (part_real * factor_imag[:, :, None] + part_imag * factor_real[:, :, None]) * inverse_root
    return jnp.concatenate([out_real, out_imag], axis=1)

def reference(snapshots, weights, reference_field, start_basis):
    dft_rows = dft_table()
    block_count = NROWS // ROW_DEV
    root_all = jnp.sqrt(weights)
    probe_all = (root_all * reference_field).astype(jnp.bfloat16)
    indices = jnp.arange(block_count, dtype=jnp.int32)

    def block_coeffs(block_index):
        first_row = block_index * ROW_DEV
        rows_block = lax.dynamic_slice_in_dim(snapshots, first_row, ROW_DEV, 1)
        root_block = lax.dynamic_slice_in_dim(root_all, first_row, ROW_DEV, 0)
        probe_block = lax.dynamic_slice_in_dim(probe_all, first_row, ROW_DEV, 0)
        return (transform(rows_block, root_block, dft_rows), root_block, probe_block)

    def gram_step(current, block_index):
        coeffs, root_block, probe_block = block_coeffs(block_index)
        coeffs_wide = coeffs.astype(jnp.float32)
        real_part = jnp.einsum('fpbx,fpcx->fbc', coeffs_wide, coeffs_wide, precision=highest)
        cross_part = jnp.einsum('fbx,fcx->fbc', coeffs_wide[:, 0], coeffs_wide[:, 1], precision=highest)
        gram_real = current[0] + real_part
        gram_imag = current[1] + (cross_part - jnp.swapaxes(cross_part, 1, 2))
        correlation = current[2] + jnp.einsum('fpbx,x->fpb', coeffs_wide, probe_block.astype(jnp.float32), precision=highest)
        return ((gram_real, gram_imag, correlation), None)
    zeros_gram = jnp.zeros((NF, NBLK, NBLK), jnp.float32)
    totals, leftover = lax.scan(gram_step, (zeros_gram, zeros_gram, jnp.zeros((NF, 2, NBLK), jnp.float32)), indices)
    gram_real = totals[0] / NROWS
    gram_imag = totals[1] / NROWS
    projection = totals[2] / math.sqrt(NROWS)
    basis_real, basis_imag, energy = subspace_solve(gram_real, gram_imag, start_basis)
    coef_matrix = coefficient_matrix(basis_real, basis_imag)
    coef_wide = coef_matrix.astype(jnp.float32)
    correlation = jnp.einsum('fpb,fpbk->fk', projection, coef_wide, precision=highest)
    factor_real, factor_imag = phase_turn(correlation, energy)

    def mode_block(block_index):
        coeffs, root_block, probe_block = block_coeffs(block_index)
        projected = jnp.einsum('fpbk,fpbx->fkx', coef_wide, coeffs.astype(jnp.float32), precision=highest)
        return finish(projected, factor_real, factor_imag, root_block)
    mode_blocks = lax.map(mode_block, indices)
    spod_modes = jnp.transpose(mode_blocks, (1, 2, 0, 3)).reshape(NF, 2 * NM, NROWS)
    return (spod_modes, energy)
```

```python
import math

import numpy as np
import jax
import jax.numpy as jnp
from jax import lax
from jax.experimental import pallas as pl
from jax.experimental.pallas import tpu as pltpu
from jax.sharding import PartitionSpec as P

NFFT = 256
NBLK = 63
NF = 64
NM = 8
ITERS = 12
XC = 256


def dft_table():
    steps = np.arange(NFFT, dtype=np.int32)
    bins = np.arange(1, NF + 1, dtype=np.int32)
    wrapped = bins[:, None] * steps[None, :] % NFFT
    angles = np.float32(2.0 * math.pi / NFFT) * wrapped.astype(np.float32)
    taper = np.float32(0.5) - np.float32(0.5) * np.cos(
        np.float32(2.0 * math.pi / NFFT) * steps.astype(np.float32)
    )
    scaled = taper / np.sqrt(np.sum(taper * taper))
    stacked = np.stack([np.cos(angles), -np.sin(angles)]) * scaled[None, None, :]
    return stacked.astype(jnp.bfloat16)


def pair_tables():
    rows = dft_table().reshape(2 * NF, NFFT)
    tables = np.zeros((8, 256, 384), rows.dtype)
    for r in range(8):
        for g in range(16):
            for w in range(8):
                source = rows[8 * g + (w - r) % 8]
                tables[r, 16 * g + 2 * w, :256] = source
                tables[r, 16 * g + 2 * w + 1, 128:] = source
    return tables


def transform_kernel(snap_ref, table_ref, root_ref, probe_ref, coeff_ref, gram_ref, buf, stage, sems):
    pieces = 4
    piece_rows = snap_ref.shape[0] // pieces
    chunks = snap_ref.shape[1] // XC
    rows = snap_ref.shape[0]

    def piece_copy(chunk, slot, piece):
        lanes = pl.ds(pl.multiple_of(chunk * XC, XC), XC)
        span = pl.ds(piece * piece_rows, piece_rows)
        return pltpu.make_async_copy(
            snap_ref.at[span, lanes], buf.at[slot, span, :], sems.at[slot, piece]
        )

    for piece in range(pieces):
        piece_copy(0, 0, piece).start()
    for slot in range(2):
        buf[slot, rows:, :] = jnp.zeros((128, XC), jnp.bfloat16)
    word = lax.broadcasted_iota(jnp.int32, (16, XC), 0) // 2
    odd_row = lax.broadcasted_iota(jnp.int32, (256, XC), 0)
    is_odd = odd_row % 2 == 1
    real_half = odd_row < 128
    bits = [(word // s) % 2 == 1 for s in (1, 2, 4)]

    def step(s, carry):
        chunk, group = s // 4, s % 4
        slot = chunk % 2
        lanes = pl.ds(pl.multiple_of(chunk * XC, XC), XC)

        @pl.when(jnp.logical_and(group == 0, chunk + 1 < chunks))
        def _():
            for piece in range(pieces):
                piece_copy(chunk + 1, 1 - slot, piece).start()

        @pl.when(group == 0)
        def _():
            piece_copy(chunk, slot, 0).wait()
            piece_copy(chunk, slot, 1).wait()

        @pl.when(group == 1)
        def _():
            piece_copy(chunk, slot, 2).wait()

        @pl.when(group == 2)
        def _():
            piece_copy(chunk, slot, 3).wait()

        root = root_ref[:, lanes]
        for r in range(8):
            first = pl.multiple_of((group * 8 + r) * 256, 256)
            out = jnp.dot(
                table_ref[r], buf[slot, pl.ds(first, 384), :], preferred_element_type=jnp.float32
            )
            out = out * root
            if r == 7:
                probe = jnp.where(real_half, probe_ref[:, lanes], 0.0)
                out = jnp.where(jnp.logical_and(is_odd, group == 3), probe, out)
            stage[r] = out.astype(jnp.bfloat16)
        for g in range(16):
            tiles = [stage[r, 16 * g : 16 * g + 16, :] for r in range(8)]
            for level, bit in zip((1, 2, 4), bits):
                tiles = [jnp.where(bit, tiles[(m + level) % 8], tiles[m]) for m in range(8)]
            part, base = g // 8, 8 * (g % 8)
            for i in range(8):
                place = pl.ds(pl.multiple_of(part * 64 + group * 16, 16), 16)
                coeff_ref[base + i, place, lanes] = tiles[(-i) % 8]
        return carry

    lax.fori_loop(0, chunks * 4, step, 0)

    row = lax.broadcasted_iota(jnp.int32, (64, 128), 0)
    lane = lax.broadcasted_iota(jnp.int32, (64, 128), 1)
    left = lane < 64
    sign = jnp.where(left, 1.0, -1.0)
    upper = row <= lane % 64

    def gram(f, carry):
        block = coeff_ref[f]
        full = lax.dot_general(
            block, block, (((1,), (1,)), ((), ())), preferred_element_type=jnp.float32
        )
        packed = full[:64] + pltpu.roll(full[64:], 64, 1) * sign
        turned = pltpu.roll(packed, 64, 1)
        top = jnp.where(upper, packed, turned)
        bottom = jnp.where(upper, turned, packed)
        gram_ref[f] = jnp.where(left[:32], top[:32], bottom[32:])
        return carry

    lax.fori_loop(0, NF, gram, 0)


def transform(snapshots, root, probe, tables):
    rows, lanes = snapshots.shape
    vmem = pl.BlockSpec(memory_space=pltpu.VMEM)
    return pl.pallas_call(
        transform_kernel,
        out_shape=(
            jax.ShapeDtypeStruct((NF, 128, lanes), jnp.bfloat16),
            jax.ShapeDtypeStruct((NF, 32, 128), jnp.float32),
        ),
        in_specs=[pl.BlockSpec(memory_space=pl.ANY), vmem, vmem, vmem],
        out_specs=(vmem, vmem),
        scratch_shapes=[
            pltpu.VMEM((2, rows + 128, XC), jnp.bfloat16),
            pltpu.VMEM((8, 256, XC), jnp.bfloat16),
            pltpu.SemaphoreType.DMA((2, 4)),
        ],
        compiler_params=pltpu.CompilerParams(vmem_limit_bytes=60000 * 1024),
        name="transform",
    )(snapshots, tables, root, probe)


def split3(x):
    first = x.astype(jnp.bfloat16).astype(jnp.float32)
    rest = x - first
    second = rest.astype(jnp.bfloat16).astype(jnp.float32)
    return first, second, rest - second


def solve_tile(packed, start, pad, total_rows):
    row = lax.broadcasted_iota(jnp.int32, (64, 128), 0)
    lane = lax.broadcasted_iota(jnp.int32, (64, 128), 1)
    left = lane < 64
    stacked = jnp.concatenate([packed, pltpu.roll(packed, 64, 1)], axis=0)
    stacked = jnp.where(left, stacked, 0.0)
    square = jnp.concatenate([stacked, jnp.zeros_like(stacked)], axis=0)
    flipped = jnp.transpose(square)[:64]
    real = jnp.where(row <= lane, stacked, flipped)
    imag = jnp.where(row > lane, stacked, jnp.where(row < lane, -flipped, 0.0))
    real = jnp.where(left, real, 0.0)
    imag = jnp.where(left, imag, 0.0)
    at_pad = row == pad
    root_total = 1.0 / math.sqrt(total_rows)
    proj_real = jnp.sum(jnp.where(at_pad, real, 0.0), axis=0, keepdims=True) * root_total
    proj_imag = jnp.sum(jnp.where(at_pad, imag, 0.0), axis=0, keepdims=True) * root_total
    inside = jnp.logical_and(jnp.logical_not(at_pad), lane != pad)
    inside_line = lax.broadcasted_iota(jnp.int32, (1, 128), 1) != pad
    proj_real = jnp.where(inside_line, proj_real, 0.0)
    proj_imag = jnp.where(inside_line, proj_imag, 0.0)
    real = jnp.where(inside, real, 0.0) * (1.0 / total_rows)
    imag = jnp.where(inside, imag, 0.0) * (1.0 / total_rows)
    weight = jnp.concatenate(
        [real - pltpu.roll(imag, 64, 1), imag + pltpu.roll(real, 64, 1)], axis=0
    )
    w1, w2, w3 = split3(weight)
    wide = jnp.concatenate([w1, w2, w3], axis=1).astype(jnp.bfloat16)
    left8 = lax.broadcasted_iota(jnp.int32, (8, 128), 1) < 64
    sign8 = jnp.where(left8, 1.0, -1.0)
    row8 = lax.broadcasted_iota(jnp.int32, (8, 128), 0)

    def image(v):
        v1, v2, v3 = split3(v)
        stack = jnp.concatenate([v1, v2, v3, jnp.zeros_like(v3)], axis=0).astype(jnp.bfloat16)
        out = jnp.dot(stack, wide, preferred_element_type=jnp.float32)
        small = out[:8, 256:] + out[8:16, 128:256] + out[16:24, :128]
        return (small + (out[:8, 128:256] + out[8:16, :128])) + out[:8, :128]

    def total(x):
        return jnp.sum(x, axis=1, keepdims=True)

    def sweep(index, v):
        y = image(v)
        x = pltpu.roll(y, 64, 1) * sign8
        norms = jnp.zeros((8, 128), jnp.float32)
        for j in range(NM):
            yj = jnp.broadcast_to(y[j : j + 1], (8, 128))
            c_real = jnp.broadcast_to(total(yj * y), (8, 128))
            norm = jnp.broadcast_to(c_real[j : j + 1], (8, 128)) + 1e-06
            norms = jnp.where(row8 == j, norm, norms)
            if j + 1 < NM:
                xj = jnp.broadcast_to(x[j : j + 1], (8, 128))
                c_imag = jnp.broadcast_to(total(yj * x), (8, 128))
                scale = jnp.where(row8 > j, 1.0 / norm, 0.0)
                a, b = c_real * scale, c_imag * scale
                y, x = y - (a * yj - b * xj), x - (a * xj + b * yj)
        return y / jnp.sqrt(norms)

    basis = lax.fori_loop(0, ITERS, sweep, start)
    energy = total(basis * image(basis))
    coef = basis.astype(jnp.bfloat16).astype(jnp.float32)
    proj_one = proj_real - pltpu.roll(proj_imag, 64, 1)
    proj_two = proj_imag + pltpu.roll(proj_real, 64, 1)
    corr_real = total(coef * proj_one)
    corr_imag = total(coef * proj_two)
    gain = 1.0 / jnp.sqrt(energy + 1e-06)
    tilt_real = gain * corr_real
    tilt_imag = gain * corr_imag
    size = jnp.sqrt(jnp.maximum(tilt_real * tilt_real + tilt_imag * tilt_imag, 0.25))
    factor_real = gain * tilt_real / size
    factor_imag = -gain * tilt_imag / size
    lane8 = lax.broadcasted_iota(jnp.int32, (8, 128), 1)
    facts = jnp.where(lane8 == 0, factor_real, jnp.where(lane8 == 1, factor_imag, energy))
    rotated = pltpu.roll(coef, 64, 1)
    rows16 = jnp.concatenate([coef * sign8, rotated], axis=0).astype(jnp.bfloat16)
    return rows16, facts


def solve_kernel(total_rows, pad_ref, gram_ref, start_ref, rows_ref, facts_ref):
    rows16, facts = solve_tile(gram_ref[...], start_ref[...], pad_ref[0], total_rows)
    rows_ref[...] = rows16
    facts_ref[...] = facts


def solve(total_rows, pad, packed, start):
    vmem = pl.BlockSpec(memory_space=pltpu.VMEM)
    return pl.pallas_call(
        lambda *refs: solve_kernel(total_rows, *refs),
        out_shape=(
            jax.ShapeDtypeStruct((16, 128), jnp.bfloat16),
            jax.ShapeDtypeStruct((8, 128), jnp.float32),
        ),
        in_specs=[pl.BlockSpec(memory_space=pltpu.SMEM), vmem, vmem],
        out_specs=(vmem, vmem),
        name="subspace",
    )(pad, packed, start)


def project_kernel(coeff_ref, rows_ref, facts_ref, inverse_ref, out_ref):
    inverse = inverse_ref[...]
    for i in range(coeff_ref.shape[0]):
        image = jnp.dot(rows_ref[i], coeff_ref[i], preferred_element_type=jnp.float32)
        real, imag = image[:8], image[8:]
        turn_real, turn_imag = facts_ref[i, :, 0:1], facts_ref[i, :, 1:2]
        out_ref[i, :8] = (real * turn_real - imag * turn_imag) * inverse
        out_ref[i, 8:] = (real * turn_imag + imag * turn_real) * inverse


def project(coeffs, rows16, facts, inverse):
    lanes = coeffs.shape[2]
    step = 8
    return pl.pallas_call(
        project_kernel,
        grid=(NF // step,),
        out_shape=jax.ShapeDtypeStruct((NF, 2 * NM, lanes), jnp.float32),
        in_specs=[
            pl.BlockSpec((step, 128, lanes), lambda i: (i, 0, 0)),
            pl.BlockSpec((step, 16, 128), lambda i: (i, 0, 0)),
            pl.BlockSpec((step, 8, 128), lambda i: (i, 0, 0)),
            pl.BlockSpec((1, lanes), lambda i: (0, 0)),
        ],
        out_specs=pl.BlockSpec((step, 16, lanes), lambda i: (i, 0, 0)),
        compiler_params=pltpu.CompilerParams(vmem_limit_bytes=24 << 20),
        name="project",
    )(coeffs, rows16, facts, inverse)


def start_rows(start_basis):
    padded = jnp.pad(start_basis, ((0, 0), (0, 0), (0, 1), (0, 0)))
    lined = jnp.transpose(padded, (0, 3, 1, 2)).reshape(NF // 8, 8, NM, 2, 4, 8, 2)
    turned = [jnp.roll(lined[:, i], i, axis=4) for i in range(8)]
    return jnp.stack(turned, axis=1).reshape(NF, NM, 128)


def shards(snapshots, weights, reference_field, start_basis):
    axes = ("grp", "row")
    total_rows = snapshots.shape[1] * lax.axis_size(axes)
    root_weight = jnp.sqrt(weights)
    root = root_weight[None]
    probe = (root_weight * reference_field)[None]
    tables = jnp.asarray(pair_tables())
    coeffs, packed = transform(snapshots, root, probe, tables)
    summed = lax.psum(packed, axes)
    mine = lax.axis_index(axes) // 2
    own = lax.dynamic_index_in_dim(summed, mine, 0, keepdims=False)
    start = lax.dynamic_index_in_dim(start_rows(start_basis), mine, 0, keepdims=False)
    pad = jnp.reshape(48 + 2 * ((7 + mine) % 8) + 1, (1,)).astype(jnp.int32)
    rows16, facts = solve(total_rows, pad, own, start)
    rows16 = lax.all_gather(rows16, axes).reshape(NF, 2, 16, 128)[:, 0]
    facts = lax.all_gather(facts, axes).reshape(NF, 2, 8, 128)[:, 0]
    modes = project(coeffs, rows16, facts, 1.0 / root)
    return modes, facts[:, :, 2]


def solution(mesh):
    in_specs = (P(None, ("grp", "row")), P(("grp", "row")), P(("grp", "row")), P())
    out_specs = (P(None, None, ("grp", "row")), P())
    return jax.shard_map(shards, mesh=mesh, in_specs=in_specs, out_specs=out_specs, check_vma=False)
```

```python
import functools
import math

import numpy as np
import jax
import jax.numpy as jnp
from jax import lax
from jax.experimental import pallas as pl
from jax.experimental.pallas import tpu as pltpu
from jax.sharding import PartitionSpec as P

NFFT = 256
NBLK = 63
NF = 64
NM = 8
ITERS = 12
XC = 256
MESH = pl.DeviceIdType.MESH


def dft_table():
    steps = np.arange(NFFT, dtype=np.int32)
    bins = np.arange(1, NF + 1, dtype=np.int32)
    wrapped = bins[:, None] * steps[None, :] % NFFT
    angles = np.float32(2.0 * math.pi / NFFT) * wrapped.astype(np.float32)
    taper = np.float32(0.5) - np.float32(0.5) * np.cos(
        np.float32(2.0 * math.pi / NFFT) * steps.astype(np.float32)
    )
    scaled = taper / np.sqrt(np.sum(taper * taper))
    stacked = np.stack([np.cos(angles), -np.sin(angles)]) * scaled[None, None, :]
    return stacked.astype(jnp.bfloat16)


def pair_tables():
    rows = dft_table().reshape(2 * NF, NFFT)
    tables = np.zeros((8, 256, 384), rows.dtype)
    for r in range(8):
        for g in range(16):
            for w in range(8):
                source = rows[8 * g + (w - r) % 8]
                tables[r, 16 * g + 2 * w, :256] = source
                tables[r, 16 * g + 2 * w + 1, 128:] = source
    return tables


def packed_masks():
    row = lax.broadcasted_iota(jnp.int32, (64, 128), 0)
    lane = lax.broadcasted_iota(jnp.int32, (64, 128), 1)
    left = lane < 64
    return left, jnp.where(left, 1.0, -1.0), row <= lane % 64


def transform_kernel(
    total_rows, devices, inner,
    snap_ref, table_ref, weight_ref, field_ref, start_ref,
    coeff_ref, share_ref,
    buf, stage, gram_ref, slots, snap_sems, sum_send, sum_recv, share_send, share_recv,
):
    pieces = 4
    piece_rows = snap_ref.shape[0] // pieces
    chunks = snap_ref.shape[1] // XC
    rows = snap_ref.shape[0]
    grp, row = lax.axis_index("grp"), lax.axis_index("row")
    me = grp * inner + row
    mine = me // 2
    is_owner = row % 2 == mine % 2

    def device(index):
        return (index // inner, index % inner)

    barrier = pltpu.get_barrier_semaphore()

    def greet(k, carry):
        pl.semaphore_signal(barrier, inc=1, device_id=device((me + k) % devices), device_id_type=MESH)
        return carry

    def piece_copy(chunk, slot, piece):
        lanes = pl.ds(pl.multiple_of(chunk * XC, XC), XC)
        span = pl.ds(piece * piece_rows, piece_rows)
        return pltpu.make_async_copy(
            snap_ref.at[span, lanes], buf.at[slot, span, :], snap_sems.at[slot, piece]
        )

    for piece in range(pieces):
        piece_copy(0, 0, piece).start()
    lax.fori_loop(1, devices, greet, 0)
    for slot in range(2):
        buf[slot, rows:, :] = jnp.zeros((128, XC), jnp.bfloat16)
    word = lax.broadcasted_iota(jnp.int32, (16, XC), 0) // 2
    odd_row = lax.broadcasted_iota(jnp.int32, (256, XC), 0)
    is_odd = odd_row % 2 == 1
    real_half = odd_row < 128
    bits = [(word // s) % 2 == 1 for s in (1, 2, 4)]

    def step(s, carry):
        chunk, group = s // 4, s % 4
        slot = chunk % 2
        lanes = pl.ds(pl.multiple_of(chunk * XC, XC), XC)

        @pl.when(jnp.logical_and(group == 0, chunk + 1 < chunks))
        def _():
            for piece in range(pieces):
                piece_copy(chunk + 1, 1 - slot, piece).start()

        @pl.when(group == 0)
        def _():
            piece_copy(chunk, slot, 0).wait()
            piece_copy(chunk, slot, 1).wait()

        @pl.when(group == 1)
        def _():
            piece_copy(chunk, slot, 2).wait()

        @pl.when(group == 2)
        def _():
            piece_copy(chunk, slot, 3).wait()

        root = jnp.sqrt(weight_ref[:, lanes])
        for r in range(8):
            first = pl.multiple_of((group * 8 + r) * 256, 256)
            out = jnp.dot(
                table_ref[r], buf[slot, pl.ds(first, 384), :], preferred_element_type=jnp.float32
            )
            out = out * root
            if r == 7:
                probe = jnp.where(real_half, root * field_ref[:, lanes], 0.0)
                out = jnp.where(jnp.logical_and(is_odd, group == 3), probe, out)
            stage[r] = out.astype(jnp.bfloat16)
        for g in range(16):
            tiles = [stage[r, 16 * g : 16 * g + 16, :] for r in range(8)]
            for level, bit in zip((1, 2, 4), bits):
                tiles = [jnp.where(bit, tiles[(m + level) % 8], tiles[m]) for m in range(8)]
            part, base = g // 8, 8 * (g % 8)
            for i in range(8):
                place = pl.ds(pl.multiple_of(part * 64 + group * 16, 16), 16)
                coeff_ref[base + i, place, lanes] = tiles[(-i) % 8]
        return carry

    lax.fori_loop(0, chunks * 4, step, 0)
    pl.semaphore_wait(barrier, devices - 1)
    left, sign, upper = packed_masks()

    def gram(f):
        block = coeff_ref[f]
        full = lax.dot_general(
            block, block, (((1,), (1,)), ((), ())), preferred_element_type=jnp.float32
        )
        packed = full[:64] + pltpu.roll(full[64:], 64, 1) * sign
        turned = pltpu.roll(packed, 64, 1)
        top = jnp.where(upper, packed, turned)
        bottom = jnp.where(upper, turned, packed)
        gram_ref[f] = jnp.where(left[:32], top[:32], bottom[32:])

    def give(f):
        owner = 2 * f + f % 2
        return pltpu.make_async_remote_copy(
            src_ref=gram_ref.at[f],
            dst_ref=slots.at[me],
            send_sem=sum_send,
            recv_sem=sum_recv,
            device_id=device(owner),
            device_id_type=MESH,
        )

    def gram_step(i, carry):
        gram((mine + 1 + i) % NF)

        @pl.when(i > 0)
        def _():
            give((mine + i) % NF).start()

        return carry

    lax.fori_loop(0, NF, gram_step, 0)
    pad = 48 + 2 * ((7 + mine) % 8) + 1

    def all_of(ref, count, sem):
        part = ref.at[pl.ds(0, count)]
        pltpu.make_async_copy(part, part, sem).wait()

    @pl.when(jnp.logical_not(is_owner))
    def _():
        give(mine).start()
        all_of(gram_ref, NF, sum_send)
        all_of(share_ref, NF, share_recv)

    @pl.when(is_owner)
    def _():
        slots[me] = gram_ref[mine]
        start = start_tile(start_ref, mine)
        all_of(slots, devices - 1, sum_recv)

        def add(i, total):
            for j in range(8):
                total = total + slots[i * 8 + j]
            return total

        packed = lax.fori_loop(0, devices // 8, add, jnp.zeros((32, 128), jnp.float32))
        share_ref[mine] = solve_tile(packed, start, pad, total_rows)
        all_of(gram_ref, NF - 1, sum_send)

        def share(k, carry):
            pltpu.make_async_remote_copy(
                src_ref=share_ref.at[mine],
                dst_ref=share_ref.at[mine],
                send_sem=share_send,
                recv_sem=share_recv,
                device_id=device((me + k) % devices),
                device_id_type=MESH,
            ).start()
            return carry

        lax.fori_loop(1, devices, share, 0)
        all_of(share_ref, NF - 1, share_recv)
        for count in (NF, devices - 1 - NF):
            all_of(share_ref, count, share_send)


def start_tile(start_ref, mine):
    lane = lax.broadcasted_iota(jnp.int32, (8, 128), 1)
    ours = lax.broadcasted_iota(jnp.int32, (8, NF), 1) == mine
    tile = jnp.zeros((8, 128), jnp.float32)

    def one(b, tile):
        word, e = b // 2, b % 2
        place = 16 * (word // 8) + 2 * ((word % 8 + mine) % 8) + e
        for p in range(2):
            column = jnp.sum(jnp.where(ours, start_ref[p, b], 0.0), axis=1, keepdims=True)
            tile = jnp.where(lane == 64 * p + place, column, tile)
        return tile

    return lax.fori_loop(0, NBLK, one, tile)


def transform(total_rows, devices, inner, snapshots, tables, weights, field, start):
    rows, lanes = snapshots.shape
    vmem = pl.BlockSpec(memory_space=pltpu.VMEM)
    return pl.pallas_call(
        functools.partial(transform_kernel, total_rows, devices, inner),
        out_shape=(
            pltpu.VMEM((NF, 128, lanes), jnp.bfloat16),
            pltpu.VMEM((NF, 16, 128), jnp.float32),
        ),
        in_specs=[pl.BlockSpec(memory_space=pltpu.HBM), vmem, vmem, vmem, vmem],
        out_specs=(vmem, vmem),
        scratch_shapes=[
            pltpu.VMEM((2, rows + 128, XC), jnp.bfloat16),
            pltpu.VMEM((8, 256, XC), jnp.bfloat16),
            pltpu.VMEM((NF, 32, 128), jnp.float32),
            pltpu.VMEM((devices, 32, 128), jnp.float32),
            pltpu.SemaphoreType.DMA((2, 4)),
            pltpu.SemaphoreType.DMA,
            pltpu.SemaphoreType.DMA,
            pltpu.SemaphoreType.DMA,
            pltpu.SemaphoreType.DMA,
        ],
        compiler_params=pltpu.CompilerParams(
            vmem_limit_bytes=32 << 20, collective_id=0, has_side_effects=True
        ),
        name="transform",
    )(snapshots, tables, weights, field, start)


def split3(x):
    first = x.astype(jnp.bfloat16).astype(jnp.float32)
    rest = x - first
    second = rest.astype(jnp.bfloat16).astype(jnp.float32)
    return first, second, rest - second


def solve_tile(packed, start, pad, total_rows):
    row = lax.broadcasted_iota(jnp.int32, (64, 128), 0)
    lane = lax.broadcasted_iota(jnp.int32, (64, 128), 1)
    left = lane < 64
    stacked = jnp.concatenate([packed, pltpu.roll(packed, 64, 1)], axis=0)
    stacked = jnp.where(left, stacked, 0.0)
    square = jnp.concatenate([stacked, jnp.zeros_like(stacked)], axis=0)
    flipped = jnp.transpose(square)[:64]
    real = jnp.where(row <= lane, stacked, flipped)
    imag = jnp.where(row > lane, stacked, jnp.where(row < lane, -flipped, 0.0))
    real = jnp.where(left, real, 0.0)
    imag = jnp.where(left, imag, 0.0)
    at_pad = row == pad
    root_total = 1.0 / math.sqrt(total_rows)
    proj_real = jnp.sum(jnp.where(at_pad, real, 0.0), axis=0, keepdims=True) * root_total
    proj_imag = jnp.sum(jnp.where(at_pad, imag, 0.0), axis=0, keepdims=True) * root_total
    inside = jnp.logical_and(jnp.logical_not(at_pad), lane != pad)
    inside_line = lax.broadcasted_iota(jnp.int32, (1, 128), 1) != pad
    proj_real = jnp.where(inside_line, proj_real, 0.0)
    proj_imag = jnp.where(inside_line, proj_imag, 0.0)
    real = jnp.where(inside, real, 0.0) * (1.0 / total_rows)
    imag = jnp.where(inside, imag, 0.0) * (1.0 / total_rows)
    weight = jnp.concatenate(
        [real - pltpu.roll(imag, 64, 1), imag + pltpu.roll(real, 64, 1)], axis=0
    )
    w1, w2, w3 = split3(weight)
    wide = jnp.concatenate([w1, w2, w3], axis=1).astype(jnp.bfloat16)
    left8 = lax.broadcasted_iota(jnp.int32, (8, 128), 1) < 64
    sign8 = jnp.where(left8, 1.0, -1.0)
    row8 = lax.broadcasted_iota(jnp.int32, (8, 128), 0)

    def image(v):
        v1, v2, v3 = split3(v)
        stack = jnp.concatenate([v1, v2, v3, jnp.zeros_like(v3)], axis=0).astype(jnp.bfloat16)
        out = jnp.dot(stack, wide, preferred_element_type=jnp.float32)
        small = out[:8, 256:] + out[8:16, 128:256] + out[16:24, :128]
        return (small + (out[:8, 128:256] + out[8:16, :128])) + out[:8, :128]

    def total(x):
        return jnp.sum(x, axis=1, keepdims=True)

    def sweep(index, v):
        y = image(v)
        x = pltpu.roll(y, 64, 1) * sign8
        norms = jnp.zeros((8, 128), jnp.float32)
        for j in range(NM):
            yj = jnp.broadcast_to(y[j : j + 1], (8, 128))
            c_real = jnp.broadcast_to(total(yj * y), (8, 128))
            norm = jnp.broadcast_to(c_real[j : j + 1], (8, 128)) + 1e-06
            norms = jnp.where(row8 == j, norm, norms)
            if j + 1 < NM:
                xj = jnp.broadcast_to(x[j : j + 1], (8, 128))
                c_imag = jnp.broadcast_to(total(yj * x), (8, 128))
                scale = jnp.where(row8 > j, 1.0 / norm, 0.0)
                a, b = c_real * scale, c_imag * scale
                y, x = y - (a * yj - b * xj), x - (a * xj + b * yj)
        return y / jnp.sqrt(norms)

    basis = lax.fori_loop(0, ITERS, sweep, start)
    energy = total(basis * image(basis))
    coef = basis.astype(jnp.bfloat16).astype(jnp.float32)
    proj_one = proj_real - pltpu.roll(proj_imag, 64, 1)
    proj_two = proj_imag + pltpu.roll(proj_real, 64, 1)
    corr_real = total(coef * proj_one)
    corr_imag = total(coef * proj_two)
    gain = 1.0 / jnp.sqrt(energy + 1e-06)
    tilt_real = gain * corr_real
    tilt_imag = gain * corr_imag
    size = jnp.sqrt(jnp.maximum(tilt_real * tilt_real + tilt_imag * tilt_imag, 0.25))
    factor_real = gain * tilt_real / size
    factor_imag = -gain * tilt_imag / size
    lane8 = lax.broadcasted_iota(jnp.int32, (8, 128), 1)
    facts = jnp.where(lane8 == 0, factor_real, jnp.where(lane8 == 1, factor_imag, energy))
    return jnp.concatenate([coef, facts], axis=0)


def project_kernel(coeff_ref, share_ref, weight_ref, out_ref, energy_ref):
    inverse = 1.0 / jnp.sqrt(weight_ref[...])
    lane = lax.broadcasted_iota(jnp.int32, (8, 128), 1)
    sign = jnp.where(lane < 64, 1.0, -1.0)
    place = lax.broadcasted_iota(jnp.int32, (8, NF), 1)
    step = out_ref.shape[0]
    first = pl.program_id(0) * step
    energies = energy_ref[...]
    for i in range(step):
        coef = share_ref[first + i, :8]
        rows16 = jnp.concatenate([coef * sign, pltpu.roll(coef, 64, 1)], axis=0)
        image = jnp.dot(
            rows16.astype(jnp.bfloat16), coeff_ref[first + i], preferred_element_type=jnp.float32
        )
        real, imag = image[:8], image[8:]
        turn_real, turn_imag = share_ref[first + i, 8:, 0:1], share_ref[first + i, 8:, 1:2]
        out_ref[i, :8] = (real * turn_real - imag * turn_imag) * inverse
        out_ref[i, 8:] = (real * turn_imag + imag * turn_real) * inverse
        energies = jnp.where(place == first + i, share_ref[first + i, 8:, 2:3], energies)
    energy_ref[...] = energies


def project(coeffs, shares, weights):
    lanes = coeffs.shape[2]
    step = 8
    vmem = pl.BlockSpec(memory_space=pltpu.VMEM)
    return pl.pallas_call(
        project_kernel,
        grid=(NF // step,),
        out_shape=(
            jax.ShapeDtypeStruct((NF, 2 * NM, lanes), jnp.float32),
            jax.ShapeDtypeStruct((NM, NF), jnp.float32),
        ),
        in_specs=[vmem, vmem, pl.BlockSpec((1, lanes), lambda i: (0, 0))],
        out_specs=(
            pl.BlockSpec((step, 16, lanes), lambda i: (i, 0, 0)),
            pl.BlockSpec((NM, NF), lambda i: (0, 0)),
        ),
        compiler_params=pltpu.CompilerParams(vmem_limit_bytes=6 << 20),
        name="project",
    )(coeffs, shares, weights)


def shards(snapshots, weights, reference_field, start_basis):
    axes = ("grp", "row")
    devices, inner = lax.axis_size(axes), lax.axis_size("row")
    total_rows = snapshots.shape[1] * devices
    start = jnp.transpose(start_basis, (1, 2, 3, 0))
    coeffs, shares = transform(
        total_rows, devices, inner,
        snapshots, jnp.asarray(pair_tables()), weights[None], reference_field[None], start,
    )
    modes, energies = project(coeffs, shares, weights[None])
    return modes, energies.T


def solution(mesh):
    in_specs = (P(None, ("grp", "row")), P(("grp", "row")), P(("grp", "row")), P())
    out_specs = (P(None, None, ("grp", "row")), P())
    return jax.shard_map(shards, mesh=mesh, in_specs=in_specs, out_specs=out_specs, check_vma=False)
```

```python
import functools
import math

import numpy as np
import jax
import jax.numpy as jnp
from jax import lax
from jax.experimental import pallas as pl
from jax.experimental.pallas import tpu as pltpu
from jax.sharding import PartitionSpec as P

NFFT = 256
NBLK = 63
NF = 64
NM = 8
ITERS = 12
XC = 256
GRAMS = 4
MESH = pl.DeviceIdType.MESH


def dft_table():
    steps = np.arange(NFFT, dtype=np.int32)
    bins = np.arange(1, NF + 1, dtype=np.int32)
    wrapped = bins[:, None] * steps[None, :] % NFFT
    angles = np.float32(2.0 * math.pi / NFFT) * wrapped.astype(np.float32)
    taper = np.float32(0.5) - np.float32(0.5) * np.cos(
        np.float32(2.0 * math.pi / NFFT) * steps.astype(np.float32)
    )
    scaled = taper / np.sqrt(np.sum(taper * taper))
    stacked = np.stack([np.cos(angles), -np.sin(angles)]) * scaled[None, None, :]
    return stacked.astype(jnp.bfloat16)


def pair_tables():
    rows = dft_table().reshape(2 * NF, NFFT)
    tables = np.zeros((8, 256, 384), rows.dtype)
    for r in range(8):
        for g in range(16):
            for w in range(8):
                source = rows[8 * g + (w - r) % 8]
                tables[r, 16 * g + 2 * w, :256] = source
                tables[r, 16 * g + 2 * w + 1, 128:] = source
    return tables


def packed_masks():
    row = lax.broadcasted_iota(jnp.int32, (64, 128), 0)
    lane = lax.broadcasted_iota(jnp.int32, (64, 128), 1)
    left = lane < 64
    return left, jnp.where(left, 1.0, -1.0), row <= lane % 64


def transform_kernel(
    total_rows, devices, inner,
    snap_ref, table_hbm, weight_hbm, field_hbm, start_hbm,
    coeff_ref, share_ref,
    buf, stage_a, stage_b, table_ref, weight_ref, field_ref, start_ref, gram_ref, pair_slots, slots,
    snap_sems, side_sems, pair_sems, sum_send, sum_recv, share_send, share_recv,
):
    pieces = 4
    piece_rows = snap_ref.shape[0] // pieces
    chunks = snap_ref.shape[1] // XC
    rows = snap_ref.shape[0]
    chips = devices // 2
    grp, row = lax.axis_index("grp"), lax.axis_index("row")
    me = grp * inner + row
    mine = lax.div(me, 2)
    core = lax.rem(me, 2)
    is_owner = core == lax.rem(mine, 2)

    def device(index):
        return (lax.div(index, inner), lax.rem(index, inner))

    barrier = pltpu.get_barrier_semaphore()

    def greet(k):
        there = lax.rem(me + k, devices)
        pl.semaphore_signal(barrier, inc=1, device_id=device(there), device_id_type=MESH)

    def piece_copy(chunk, slot, piece):
        lanes = pl.ds(pl.multiple_of(chunk * XC, XC), XC)
        span = pl.ds(piece * piece_rows, piece_rows)
        return pltpu.make_async_copy(
            snap_ref.at[span, lanes], buf.at[slot, span, :], snap_sems.at[slot, piece]
        )

    side = [
        pltpu.make_async_copy(source, target, side_sems.at[i])
        for i, (source, target) in enumerate((
            (weight_hbm, weight_ref), (field_hbm, field_ref), (table_hbm, table_ref), (start_hbm, start_ref),
        ))
    ]
    side[2].start()
    for piece in range(pieces):
        piece_copy(0, 0, piece).start()
    for i in (0, 1, 3):
        side[i].start()
    for slot in range(2):
        buf[slot, rows:, :] = jnp.zeros((128, XC), jnp.bfloat16)
    word = lax.broadcasted_iota(jnp.int32, (16, XC), 0) // 2
    row256 = lax.broadcasted_iota(jnp.int32, (256, XC), 0)
    is_odd = row256 % 2 == 1
    real_half = row256 < 128
    bits = [(word // s) % 2 == 1 for s in (1, 2, 4)]
    stages = (stage_a, stage_b)
    for i in range(4):
        side[i].wait()

    def network(source, g, group, lanes):
        tiles = [source[r, 16 * g : 16 * g + 16, :] for r in range(8)]
        for level, bit in zip((1, 2, 4), bits):
            tiles = [jnp.where(bit, tiles[(m + level) % 8], tiles[m]) for m in range(8)]
        part, base = g // 8, 8 * (g % 8)
        for i in range(8):
            first = part * 64 + group * 16
            coeff_ref[base + i, first : first + 16, lanes] = tiles[(-i) % 8]

    def chunk_step(chunk, carry):
        slot = lax.rem(chunk, 2)
        lanes = pl.ds(pl.multiple_of(chunk * XC, XC), XC)
        before = pl.ds(pl.multiple_of(lax.rem(chunk + chunks - 1, chunks) * XC, XC), XC)

        @pl.when(chunk + 1 < chunks)
        def _():
            for piece in range(pieces):
                piece_copy(chunk + 1, 1 - slot, piece).start()

        root = jnp.sqrt(weight_ref[:, lanes])
        piece_copy(chunk, slot, 0).wait()
        for group in range(4):
            if group < 3:
                piece_copy(chunk, slot, group + 1).wait()
            target, source = stages[group % 2], stages[(group + 1) % 2]
            for r in range(8):
                first = (group * 8 + r) * 256
                out = jnp.dot(
                    table_ref[r], buf[slot, first : first + 384, :], preferred_element_type=jnp.float32
                )
                out = out * root
                if r == 7 and group == 3:
                    probe = jnp.where(real_half, root * field_ref[:, lanes], 0.0)
                    out = jnp.where(is_odd, probe, out)
                target[r] = out.astype(jnp.bfloat16)
                for g in (2 * r, 2 * r + 1):
                    network(source, g, (group + 3) % 4, before if group == 0 else lanes)
            for k in range(8):
                greet((chunk * 4 + group) * 8 + k + 1)
        return carry

    lax.fori_loop(0, chunks, chunk_step, 0)
    for g in range(16):
        network(stages[1], g, 3, slice((chunks - 1) * XC, chunks * XC))
    pl.semaphore_wait(barrier, chunks * 32)
    left, sign, upper = packed_masks()

    def gram(f):
        block = coeff_ref[f]
        full = lax.dot_general(
            block, block, (((1,), (1,)), ((), ())), preferred_element_type=jnp.float32
        )
        packed = full[:64] + pltpu.roll(full[64:], 64, 1) * sign
        turned = pltpu.roll(packed, 64, 1)
        top = jnp.where(upper, packed, turned)
        bottom = jnp.where(upper, turned, packed)
        return jnp.where(left[:32], top[:32], bottom[32:])

    def nth(q, parity):
        return 2 * lax.rem(lax.div(mine, 2) + 1 + q, NF // 2) + parity

    def pair_give(f):
        return pltpu.make_async_remote_copy(
            src_ref=gram_ref.at[f],
            dst_ref=pair_slots.at[lax.div(f, 2)],
            send_sem=sum_send,
            recv_sem=pair_sems.at[lax.div(f, 2)],
            device_id=device(me + 1 - 2 * core),
            device_id_type=MESH,
        )

    def give(f):
        return pltpu.make_async_remote_copy(
            src_ref=gram_ref.at[f],
            dst_ref=slots.at[mine],
            send_sem=sum_send,
            recv_sem=sum_recv,
            device_id=device(2 * f + core),
            device_id_type=MESH,
        )

    def partner_step(i, carry):
        for u in range(GRAMS):
            f = nth(i * GRAMS + u, 1 - core)
            gram_ref[f] = gram(f)

        @pl.when(i > 0)
        def _():
            for u in range(GRAMS):
                pair_give(nth((i - 1) * GRAMS + u, 1 - core)).start()

        return carry

    trips = NF // 2 // GRAMS
    lax.fori_loop(0, trips, partner_step, 0)

    def own_step(i, carry):
        for u in range(GRAMS):
            f = nth(i * GRAMS + u, core)
            half = lax.div(f, 2)
            pltpu.make_async_copy(pair_slots.at[half], pair_slots.at[half], pair_sems.at[half]).wait()
        for u in range(GRAMS):
            f = nth(i * GRAMS + u, core)
            gram_ref[f] = gram(f) + pair_slots[lax.div(f, 2)]

        @pl.when(i == 0)
        def _():
            for u in range(GRAMS):
                pair_give(nth((trips - 1) * GRAMS + u, 1 - core)).start()

        @pl.when(i > 0)
        def _():
            for u in range(GRAMS):
                give(nth((i - 1) * GRAMS + u, core)).start()

        return carry

    lax.fori_loop(0, trips, own_step, 0)
    for u in range(GRAMS - 1):
        give(nth((trips - 1) * GRAMS + u, core)).start()
    pad = 48 + 2 * lax.rem(7 + mine, 8) + 1

    def all_of(ref, count, sem):
        part = ref.at[pl.ds(0, count)]
        pltpu.make_async_copy(part, part, sem).wait()

    @pl.when(jnp.logical_not(is_owner))
    def _():
        give(nth(NF // 2 - 1, core)).start()
        all_of(gram_ref, NF, sum_send)
        all_of(share_ref, NF, share_recv)

    @pl.when(is_owner)
    def _():
        slots[mine] = gram_ref[mine]
        start = start_tile(start_ref, mine)
        all_of(slots, chips - 1, sum_recv)

        def add(i, total):
            for j in range(8):
                total = total + slots[i * 8 + j]
            return total

        packed = lax.fori_loop(0, chips // 8, add, jnp.zeros((32, 128), jnp.float32))
        share_ref[mine] = solve_tile(packed, start, pad, total_rows)
        all_of(gram_ref, NF - 1, sum_send)

        def share(k, carry):
            pltpu.make_async_remote_copy(
                src_ref=share_ref.at[mine],
                dst_ref=share_ref.at[mine],
                send_sem=share_send,
                recv_sem=share_recv,
                device_id=device(lax.rem(me + k, devices)),
                device_id_type=MESH,
            ).start()
            return carry

        lax.fori_loop(1, devices, share, 0)
        all_of(share_ref, NF - 1, share_recv)
        for count in (NF, devices - 1 - NF):
            all_of(share_ref, count, share_send)


def start_tile(start_ref, mine):
    lane = lax.broadcasted_iota(jnp.int32, (8, 128), 1)
    ours = lax.broadcasted_iota(jnp.int32, (8, NF), 1) == mine
    tile = jnp.zeros((8, 128), jnp.float32)

    def one(b, tile):
        word, e = b // 2, b % 2
        place = 16 * (word // 8) + 2 * ((word % 8 + mine) % 8) + e
        for p in range(2):
            column = jnp.sum(jnp.where(ours, start_ref[p, b], 0.0), axis=1, keepdims=True)
            tile = jnp.where(lane == 64 * p + place, column, tile)
        return tile

    return lax.fori_loop(0, NBLK, one, tile)


def transform(total_rows, devices, inner, snapshots, tables, weights, field, start):
    rows, lanes = snapshots.shape
    vmem = pl.BlockSpec(memory_space=pltpu.VMEM)
    return pl.pallas_call(
        functools.partial(transform_kernel, total_rows, devices, inner),
        out_shape=(
            pltpu.VMEM((NF, 128, lanes), jnp.bfloat16),
            pltpu.VMEM((NF, 16, 128), jnp.bfloat16),
        ),
        in_specs=[pl.BlockSpec(memory_space=pltpu.HBM)] * 5,
        out_specs=(vmem, vmem),
        scratch_shapes=[
            pltpu.VMEM((2, rows + 128, XC), jnp.bfloat16),
            pltpu.VMEM((8, 256, XC), jnp.bfloat16),
            pltpu.VMEM((8, 256, XC), jnp.bfloat16),
            pltpu.VMEM(tables.shape, tables.dtype),
            pltpu.VMEM(weights.shape, weights.dtype),
            pltpu.VMEM(field.shape, field.dtype),
            pltpu.VMEM(start.shape, start.dtype),
            pltpu.VMEM((NF, 32, 128), jnp.float32),
            pltpu.VMEM((NF // 2, 32, 128), jnp.float32),
            pltpu.VMEM((devices // 2, 32, 128), jnp.float32),
            pltpu.SemaphoreType.DMA((2, 4)),
            pltpu.SemaphoreType.DMA((4,)),
            pltpu.SemaphoreType.DMA((NF // 2,)),
            pltpu.SemaphoreType.DMA,
            pltpu.SemaphoreType.DMA,
            pltpu.SemaphoreType.DMA,
            pltpu.SemaphoreType.DMA,
        ],
        compiler_params=pltpu.CompilerParams(
            vmem_limit_bytes=48600 * 1024, collective_id=0, has_side_effects=True
        ),
        name="transform",
    )(snapshots, tables, weights, field, start)


def split3(x):
    first = x.astype(jnp.bfloat16).astype(jnp.float32)
    rest = x - first
    second = rest.astype(jnp.bfloat16).astype(jnp.float32)
    return first, second, rest - second


def solve_tile(packed, start, pad, total_rows):
    row = lax.broadcasted_iota(jnp.int32, (64, 128), 0)
    lane = lax.broadcasted_iota(jnp.int32, (64, 128), 1)
    left = lane < 64
    stacked = jnp.concatenate([packed, pltpu.roll(packed, 64, 1)], axis=0)
    stacked = jnp.where(left, stacked, 0.0)
    square = jnp.concatenate([stacked, jnp.zeros_like(stacked)], axis=0)
    flipped = jnp.transpose(square)[:64]
    real = jnp.where(row <= lane, stacked, flipped)
    imag = jnp.where(row > lane, stacked, jnp.where(row < lane, -flipped, 0.0))
    real = jnp.where(left, real, 0.0)
    imag = jnp.where(left, imag, 0.0)
    at_pad = row == pad
    root_total = 1.0 / math.sqrt(total_rows)
    proj_real = jnp.sum(jnp.where(at_pad, real, 0.0), axis=0, keepdims=True) * root_total
    proj_imag = jnp.sum(jnp.where(at_pad, imag, 0.0), axis=0, keepdims=True) * root_total
    inside = jnp.logical_and(jnp.logical_not(at_pad), lane != pad)
    inside_line = lax.broadcasted_iota(jnp.int32, (1, 128), 1) != pad
    proj_real = jnp.where(inside_line, proj_real, 0.0)
    proj_imag = jnp.where(inside_line, proj_imag, 0.0)
    real = jnp.where(inside, real, 0.0) * (1.0 / total_rows)
    imag = jnp.where(inside, imag, 0.0) * (1.0 / total_rows)
    weight = jnp.concatenate(
        [real - pltpu.roll(imag, 64, 1), imag + pltpu.roll(real, 64, 1)], axis=0
    )
    w1, w2, w3 = split3(weight)
    wide = jnp.concatenate([w1, w2, w3], axis=1).astype(jnp.bfloat16)
    left8 = lax.broadcasted_iota(jnp.int32, (8, 128), 1) < 64
    sign8 = jnp.where(left8, 1.0, -1.0)
    row8 = lax.broadcasted_iota(jnp.int32, (8, 128), 0)

    def image(v):
        v1, v2, v3 = split3(v)
        stack = jnp.concatenate([v1, v2, v3, jnp.zeros_like(v3)], axis=0).astype(jnp.bfloat16)
        out = jnp.dot(stack, wide, preferred_element_type=jnp.float32)
        small = out[:8, 256:] + out[8:16, 128:256] + out[16:24, :128]
        return (small + (out[:8, 128:256] + out[8:16, :128])) + out[:8, :128]

    def total(x):
        return jnp.sum(x, axis=1, keepdims=True)

    def scaled(y, norms):
        inverse = lax.rsqrt(norms)
        inverse = inverse * (1.5 - 0.5 * norms * inverse * inverse)
        return y * inverse

    def line(t, j):
        return jnp.broadcast_to(t[j : j + 1], (8, 128))

    def inner(t, u):
        return jnp.broadcast_to(total(t * u), (8, 128))

    def direct(v):
        y = image(v)
        x = pltpu.roll(y, 64, 1) * sign8
        norms = jnp.zeros((8, 128), jnp.float32)
        for j in range(NM):
            yj = line(y, j)
            c_real = inner(yj, y)
            norm = line(c_real, j) + 1e-06
            norms = jnp.where(row8 == j, norm, norms)
            if j + 1 < NM:
                xj = line(x, j)
                c_imag = inner(yj, x)
                scale = jnp.where(row8 > j, 1.0 / norm, 0.0)
                a, b = c_real * scale, c_imag * scale
                y, x = y - (a * yj - b * xj), x - (a * xj + b * yj)
        return scaled(y, norms)

    def sweep(index, v):
        y = image(v)
        x = pltpu.roll(y, 64, 1) * sign8
        norms = jnp.zeros((8, 128), jnp.float32)
        g_real = [inner(line(y, j), y) for j in range(NM)]
        g_imag = [inner(line(y, j), x) for j in range(NM - 1)]
        for j in range(NM):
            square_j = jnp.maximum(line(g_real[j], j), 0.0)
            norm = square_j + 1e-06
            norms = jnp.where(row8 == j, norm, norms)
            if j + 1 < NM:
                yj, xj = line(y, j), line(x, j)
                inverse = 1.0 / norm
                scale = jnp.where(row8 > j, inverse, 0.0)
                a, b = g_real[j] * scale, g_imag[j] * scale
                y, x = y - (a * yj - b * xj), x - (a * xj + b * yj)
                both = inverse * (2.0 - square_j * inverse)
                e_real, e_imag = g_real[j] * both, g_imag[j] * both
                for k in range(j + 1, NM):
                    c_real, c_imag = line(g_real[j], k), line(g_imag[j], k)
                    g_real[k] = g_real[k] - (c_real * e_real + c_imag * e_imag)
                    if k + 1 < NM:
                        g_imag[k] = g_imag[k] - (c_real * e_imag - c_imag * e_real)
        return scaled(y, norms)

    basis = direct(lax.fori_loop(1, ITERS - 1, sweep, direct(start)))
    energy = total(basis * image(basis))
    coef = basis.astype(jnp.bfloat16).astype(jnp.float32)
    proj_one = proj_real - pltpu.roll(proj_imag, 64, 1)
    proj_two = proj_imag + pltpu.roll(proj_real, 64, 1)
    corr_real = total(coef * proj_one)
    corr_imag = total(coef * proj_two)
    gain = 1.0 / jnp.sqrt(energy + 1e-06)
    tilt_real = gain * corr_real
    tilt_imag = gain * corr_imag
    size = jnp.sqrt(jnp.maximum(tilt_real * tilt_real + tilt_imag * tilt_imag, 0.25))
    factor_real = gain * tilt_real / size
    factor_imag = -gain * tilt_imag / size
    lane8 = lax.broadcasted_iota(jnp.int32, (8, 128), 1)
    facts = jnp.zeros((8, 128), jnp.float32)
    for i, value in enumerate((factor_real, factor_imag, energy)):
        for j, piece in enumerate(split3(jnp.broadcast_to(value, (8, 128)))):
            facts = jnp.where(lane8 == 3 * j + i, piece, facts)
    return jnp.concatenate([coef, facts], axis=0).astype(jnp.bfloat16)


def project_kernel(coeff_ref, share_ref, weight_ref, out_ref, energy_ref):
    inverse = 1.0 / jnp.sqrt(weight_ref[...])
    lane = lax.broadcasted_iota(jnp.int32, (8, 128), 1)
    sign = jnp.where(lane < 64, 1.0, -1.0)
    place = lax.broadcasted_iota(jnp.int32, (8, NF), 1)
    step = out_ref.shape[0]
    first = pl.program_id(0) * step
    energies = energy_ref[...]
    for i in range(step):
        tile = share_ref[first + i].astype(jnp.float32)
        coef, parts = tile[:8], tile[8:]
        facts = parts + pltpu.roll(parts, 125, 1) + pltpu.roll(parts, 122, 1)
        rows16 = jnp.concatenate([coef * sign, pltpu.roll(coef, 64, 1)], axis=0)
        image = jnp.dot(
            rows16.astype(jnp.bfloat16), coeff_ref[first + i], preferred_element_type=jnp.float32
        )
        real, imag = image[:8], image[8:]
        turn_real, turn_imag = facts[:, 0:1], facts[:, 1:2]
        out_ref[i, :8] = (real * turn_real - imag * turn_imag) * inverse
        out_ref[i, 8:] = (real * turn_imag + imag * turn_real) * inverse
        energies = jnp.where(place == first + i, facts[:, 2:3], energies)
    energy_ref[...] = energies


def project(coeffs, shares, weights):
    lanes = coeffs.shape[2]
    step = 8
    vmem = pl.BlockSpec(memory_space=pltpu.VMEM)
    return pl.pallas_call(
        project_kernel,
        grid=(NF // step,),
        out_shape=(
            jax.ShapeDtypeStruct((NF, 2 * NM, lanes), jnp.float32),
            jax.ShapeDtypeStruct((NM, NF), jnp.float32),
        ),
        in_specs=[vmem, vmem, pl.BlockSpec((1, lanes), lambda i: (0, 0))],
        out_specs=(
            pl.BlockSpec((step, 16, lanes), lambda i: (i, 0, 0)),
            pl.BlockSpec((NM, NF), lambda i: (0, 0)),
        ),
        compiler_params=pltpu.CompilerParams(vmem_limit_bytes=6 << 20),
        name="project",
    )(coeffs, shares, weights)


def shards(snapshots, weights, reference_field, start_basis):
    axes = ("grp", "row")
    devices, inner = lax.axis_size(axes), lax.axis_size("row")
    total_rows = snapshots.shape[1] * devices
    start = jnp.transpose(start_basis, (1, 2, 3, 0))
    coeffs, shares = transform(
        total_rows, devices, inner,
        snapshots, jnp.asarray(pair_tables()), weights[None], reference_field[None], start,
    )
    modes, energies = project(coeffs, shares, weights[None])
    return modes, energies.T


def solution(mesh):
    in_specs = (P(None, ("grp", "row")), P(("grp", "row")), P(("grp", "row")), P())
    out_specs = (P(None, None, ("grp", "row")), P())
    return jax.shard_map(shards, mesh=mesh, in_specs=in_specs, out_specs=out_specs, check_vma=False)
```

```python
import functools
import math

import numpy as np
import jax
import jax.numpy as jnp
from jax import lax
from jax.experimental import pallas as pl
from jax.experimental.pallas import tpu as pltpu
from jax.sharding import PartitionSpec as P

NFFT = 256
NBLK = 63
NF = 64
NM = 8
ITERS = 12
XC = 256
MESH = pl.DeviceIdType.MESH


def dft_table():
    steps = np.arange(NFFT, dtype=np.int32)
    bins = np.arange(1, NF + 1, dtype=np.int32)
    wrapped = bins[:, None] * steps[None, :] % NFFT
    angles = np.float32(2.0 * math.pi / NFFT) * wrapped.astype(np.float32)
    taper = np.float32(0.5) - np.float32(0.5) * np.cos(
        np.float32(2.0 * math.pi / NFFT) * steps.astype(np.float32)
    )
    scaled = taper / np.sqrt(np.sum(taper * taper))
    stacked = np.stack([np.cos(angles), -np.sin(angles)]) * scaled[None, None, :]
    return stacked.astype(jnp.bfloat16)


def pair_tables():
    rows = dft_table().reshape(2 * NF, NFFT)
    tables = np.zeros((8, 256, 384), rows.dtype)
    for r in range(8):
        for g in range(16):
            for w in range(8):
                source = rows[8 * g + (w - r) % 8]
                tables[r, 16 * g + 2 * w, :256] = source
                tables[r, 16 * g + 2 * w + 1, 128:] = source
    return tables


def packed_masks():
    row = lax.broadcasted_iota(jnp.int32, (64, 128), 0)
    lane = lax.broadcasted_iota(jnp.int32, (64, 128), 1)
    left = lane < 64
    return left, jnp.where(left, 1.0, -1.0), row <= lane % 64


def transform_kernel(
    total_rows, devices, inner,
    snap_ref, table_hbm, weight_hbm, field_hbm, start_hbm,
    coeff_ref, share_ref,
    buf, stage_a, stage_b, full_a, full_b, table_ref, weight_ref, field_ref, start_ref, gram_ref, pair_slots, slots,
    snap_sems, side_sems, pair_sems, sum_send, sum_recv, share_send, share_recv,
):
    pieces = 4
    piece_rows = snap_ref.shape[0] // pieces
    chunks = snap_ref.shape[1] // XC
    rows = snap_ref.shape[0]
    chips = devices // 2
    grp, row = lax.axis_index("grp"), lax.axis_index("row")
    me = grp * inner + row
    mine = lax.div(me, 2)
    core = lax.rem(me, 2)
    is_owner = core == lax.rem(mine, 2)

    def device(index):
        return (lax.div(index, inner), lax.rem(index, inner))

    barrier = pltpu.get_barrier_semaphore()

    side_y = lax.rem(lax.div(row, 2), 4)
    side_z = lax.div(row, 8)
    xs = [lax.rem(grp + d, 4) for d in range(4)]
    ys = [lax.rem(side_y + d, 4) for d in range(4)]
    zs = [lax.rem(side_z + d, 4) for d in range(4)]
    rows_of = {
        (z, y, c): zs[z] * 8 + ys[y] * 2 + (1 - core if c else core)
        for z in range(4) for y in range(4) for c in range(2)
    }

    def greet(there, key):
        pl.semaphore_signal(barrier, inc=1, device_id=(there, rows_of[key]), device_id_type=MESH)

    def piece_copy(chunk, slot, piece):
        lanes = pl.ds(pl.multiple_of(chunk * XC, XC), XC)
        span = pl.ds(piece * piece_rows, piece_rows)
        return pltpu.make_async_copy(
            snap_ref.at[span, lanes], buf.at[slot, span, :], snap_sems.at[slot, piece]
        )

    side = [
        pltpu.make_async_copy(source, target, side_sems.at[i])
        for i, (source, target) in enumerate((
            (weight_hbm, weight_ref), (field_hbm, field_ref), (table_hbm, table_ref), (start_hbm, start_ref),
        ))
    ]
    side[2].start()
    for piece in range(pieces):
        piece_copy(0, 0, piece).start()
    for i in (0, 1, 3):
        side[i].start()
    for slot in range(2):
        buf[slot, rows:, :] = jnp.zeros((128, XC), jnp.bfloat16)
    word = lax.broadcasted_iota(jnp.int32, (16, XC), 0) // 2
    row256 = lax.broadcasted_iota(jnp.int32, (256, XC), 0)
    is_odd = row256 % 2 == 1
    real_half = row256 < 128
    bits = [(word // s) % 2 == 1 for s in (1, 2, 4)]
    stages = (stage_a, stage_b)
    for i in range(4):
        side[i].wait()

    def network(source, g, group, lanes):
        tiles = [source[r, 16 * g : 16 * g + 16, :] for r in range(8)]
        for level, bit in zip((1, 2, 4), bits):
            tiles = [jnp.where(bit, tiles[(m + level) % 8], tiles[m]) for m in range(8)]
        part, base = g // 8, 8 * (g % 8)
        for i in range(8):
            first = part * 64 + group * 16
            coeff_ref[base + i, first : first + 16, lanes] = tiles[(-i) % 8]

    def chunk_step(chunk, carry):
        slot = lax.rem(chunk, 2)
        lanes = pl.ds(pl.multiple_of(chunk * XC, XC), XC)
        before = pl.ds(pl.multiple_of(lax.rem(chunk + chunks - 1, chunks) * XC, XC), XC)

        @pl.when(chunk + 1 < chunks)
        def _():
            for piece in range(pieces):
                piece_copy(chunk + 1, 1 - slot, piece).start()

        root = jnp.sqrt(weight_ref[:, lanes])
        for piece in range(pieces):
            piece_copy(chunk, slot, piece).wait()
        for group in range(4):
            target, source = stages[group % 2], stages[(group + 1) % 2]
            for r in range(8):
                first = (group * 8 + r) * 256
                out = jnp.dot(
                    table_ref[r], buf[slot, first : first + 384, :], preferred_element_type=jnp.float32
                )
                out = out * root
                if r == 7 and group == 3:
                    probe = jnp.where(real_half, root * field_ref[:, lanes], 0.0)
                    out = jnp.where(is_odd, probe, out)
                target[r] = out.astype(jnp.bfloat16)
                for g in (2 * r, 2 * r + 1):
                    network(source, g, (group + 3) % 4, before if group == 0 else lanes)
        there = lax.rem(grp + chunk, 4)
        for key in rows_of:
            if key != (0, 0, 0):
                greet(there, key)

        @pl.when(chunk > 0)
        def _():
            greet(there, (0, 0, 0))

        return carry

    lax.fori_loop(0, chunks, chunk_step, 0)
    for g in range(16):
        network(stages[1], g, 3, slice((chunks - 1) * XC, chunks * XC))
    pl.semaphore_wait(barrier, devices - 1)
    left, sign, upper = packed_masks()

    def owner(parity, i, u):
        far = (2, 3, 1, 0)
        turn = lax.rem(parity + side_y, 2) + 2 * (1 - u % 2)
        return xs[far[i]] * 16 + zs[far[u // 2]] * 4 + lax.rem(side_y + turn, 4)

    def gram(f):
        block = coeff_ref[f]
        return lax.dot_general(
            block, block, (((1,), (1,)), ((), ())), preferred_element_type=jnp.float32
        )

    def pack(full):
        packed = full[:64] + pltpu.roll(full[64:], 64, 1) * sign
        turned = pltpu.roll(packed, 64, 1)
        top = jnp.where(upper, packed, turned)
        bottom = jnp.where(upper, turned, packed)
        return jnp.where(left[:32], top[:32], bottom[32:])

    def pair_give(f):
        return pltpu.make_async_remote_copy(
            src_ref=gram_ref.at[f],
            dst_ref=pair_slots.at[lax.div(f, 2)],
            send_sem=sum_send,
            recv_sem=pair_sems.at[lax.div(f, 2)],
            device_id=device(me + 1 - 2 * core),
            device_id_type=MESH,
        )

    def give(f):
        return pltpu.make_async_remote_copy(
            src_ref=gram_ref.at[f],
            dst_ref=slots.at[mine],
            send_sem=sum_send,
            recv_sem=sum_recv,
            device_id=device(2 * f + core),
            device_id_type=MESH,
        )

    order = ((0, 0), (0, 1), (1, 0), (0, 2), (1, 1), (0, 3), (1, 2), (1, 3))
    batches = [
        (own, [owner(core if own else 1 - core, i, u) for u in range(8)]) for own, i in order
    ]
    fulls = (full_a, full_b)
    last = len(batches) - 1
    for t in range(len(batches) + 1):
        if t > 0 and batches[t - 1][0]:
            for f in batches[t - 1][1]:
                half = pair_slots.at[lax.div(f, 2)]
                pltpu.make_async_copy(half, half, pair_sems.at[lax.div(f, 2)]).wait()
        if t > 1:
            for f in batches[t - 2][1]:
                (give if batches[t - 2][0] else pair_give)(f).start()
        for u in range(8):
            if t <= last:
                fulls[t % 2][u] = gram(batches[t][1][u])
            if t > 0:
                own, fs = batches[t - 1]
                packed = pack(fulls[(t - 1) % 2][u])
                if own:
                    packed = packed + pair_slots[lax.div(fs[u], 2)]
                gram_ref[fs[u]] = packed
    for f in batches[last][1][:-1]:
        give(f).start()
    pad = 48 + 2 * lax.rem(7 + mine, 8) + 1

    def all_of(ref, count, sem):
        part = ref.at[pl.ds(0, count)]
        pltpu.make_async_copy(part, part, sem).wait()

    @pl.when(jnp.logical_not(is_owner))
    def _():
        give(batches[last][1][-1]).start()
        all_of(gram_ref, NF, sum_send)
        all_of(share_ref, NF, share_recv)

    @pl.when(is_owner)
    def _():
        slots[mine] = gram_ref[mine]
        start = start_tile(start_ref, mine)
        all_of(slots, chips - 1, sum_recv)

        def add(i, total):
            for j in range(8):
                total = total + slots[i * 8 + j]
            return total

        packed = lax.fori_loop(0, chips // 8, add, jnp.zeros((32, 128), jnp.float32))
        share_ref[mine] = solve_tile(packed, start, pad, total_rows)
        all_of(gram_ref, NF - 1, sum_send)

        def near(d):
            return min(d, 4 - d)

        peers = [(x, key) for x in range(4) for key in rows_of if (x, key) != (0, (0, 0, 0))]
        peers.sort(key=lambda p: -(near(p[0]) + near(p[1][0]) + near(p[1][1])))
        for x, key in peers:
            pltpu.make_async_remote_copy(
                src_ref=share_ref.at[mine],
                dst_ref=share_ref.at[mine],
                send_sem=share_send,
                recv_sem=share_recv,
                device_id=(xs[x], rows_of[key]),
                device_id_type=MESH,
            ).start()
        all_of(share_ref, NF - 1, share_recv)
        for count in (NF, devices - 1 - NF):
            all_of(share_ref, count, share_send)


def start_tile(start_ref, mine):
    lane = lax.broadcasted_iota(jnp.int32, (8, 128), 1)
    ours = lax.broadcasted_iota(jnp.int32, (8, NF), 1) == mine
    tile = jnp.zeros((8, 128), jnp.float32)

    def some(i, tile):
        for j in range(21):
            b = i * 21 + j
            word, e = lax.div(b, 2), lax.rem(b, 2)
            place = 16 * lax.div(word, 8) + 2 * lax.rem(lax.rem(word, 8) + mine, 8) + e
            for p in range(2):
                column = jnp.sum(jnp.where(ours, start_ref[p, b], 0.0), axis=1, keepdims=True)
                tile = jnp.where(lane == 64 * p + place, column, tile)
        return tile

    return lax.fori_loop(0, NBLK // 21, some, tile)


def transform(total_rows, devices, inner, snapshots, tables, weights, field, start):
    rows, lanes = snapshots.shape
    vmem = pl.BlockSpec(memory_space=pltpu.VMEM)
    return pl.pallas_call(
        functools.partial(transform_kernel, total_rows, devices, inner),
        out_shape=(
            pltpu.VMEM((NF, 128, lanes), jnp.bfloat16),
            pltpu.VMEM((NF, 16, 128), jnp.bfloat16),
        ),
        in_specs=[pl.BlockSpec(memory_space=pltpu.HBM)] * 5,
        out_specs=(vmem, vmem),
        scratch_shapes=[
            pltpu.VMEM((2, rows + 128, XC), jnp.bfloat16),
            pltpu.VMEM((8, 256, XC), jnp.bfloat16),
            pltpu.VMEM((8, 256, XC), jnp.bfloat16),
            pltpu.VMEM((8, 128, 128), jnp.float32),
            pltpu.VMEM((8, 128, 128), jnp.float32),
            pltpu.VMEM(tables.shape, tables.dtype),
            pltpu.VMEM(weights.shape, weights.dtype),
            pltpu.VMEM(field.shape, field.dtype),
            pltpu.VMEM(start.shape, start.dtype),
            pltpu.VMEM((NF, 32, 128), jnp.float32),
            pltpu.VMEM((NF // 2, 32, 128), jnp.float32),
            pltpu.VMEM((devices // 2, 32, 128), jnp.float32),
            pltpu.SemaphoreType.DMA((2, 4)),
            pltpu.SemaphoreType.DMA((4,)),
            pltpu.SemaphoreType.DMA((NF // 2,)),
            pltpu.SemaphoreType.DMA,
            pltpu.SemaphoreType.DMA,
            pltpu.SemaphoreType.DMA,
            pltpu.SemaphoreType.DMA,
        ],
        compiler_params=pltpu.CompilerParams(
            vmem_limit_bytes=48600 * 1024, collective_id=0, has_side_effects=True
        ),
        name="transform",
    )(snapshots, tables, weights, field, start)


def split3(x):
    first = x.astype(jnp.bfloat16).astype(jnp.float32)
    rest = x - first
    second = rest.astype(jnp.bfloat16).astype(jnp.float32)
    return first, second, rest - second


def solve_tile(packed, start, pad, total_rows):
    row = lax.broadcasted_iota(jnp.int32, (64, 128), 0)
    lane = lax.broadcasted_iota(jnp.int32, (64, 128), 1)
    left = lane < 64
    stacked = jnp.concatenate([packed, pltpu.roll(packed, 64, 1)], axis=0)
    stacked = jnp.where(left, stacked, 0.0)
    square = jnp.concatenate([stacked, jnp.zeros_like(stacked)], axis=0)
    flipped = jnp.transpose(square)[:64]
    real = jnp.where(row <= lane, stacked, flipped)
    imag = jnp.where(row > lane, stacked, jnp.where(row < lane, -flipped, 0.0))
    real = jnp.where(left, real, 0.0)
    imag = jnp.where(left, imag, 0.0)
    at_pad = row == pad
    root_total = 1.0 / math.sqrt(total_rows)
    proj_real = jnp.sum(jnp.where(at_pad, real, 0.0), axis=0, keepdims=True) * root_total
    proj_imag = jnp.sum(jnp.where(at_pad, imag, 0.0), axis=0, keepdims=True) * root_total
    inside = jnp.logical_and(jnp.logical_not(at_pad), lane != pad)
    inside_line = lax.broadcasted_iota(jnp.int32, (1, 128), 1) != pad
    proj_real = jnp.where(inside_line, proj_real, 0.0)
    proj_imag = jnp.where(inside_line, proj_imag, 0.0)
    real = jnp.where(inside, real, 0.0) * (1.0 / total_rows)
    imag = jnp.where(inside, imag, 0.0) * (1.0 / total_rows)
    weight = jnp.concatenate(
        [real - pltpu.roll(imag, 64, 1), imag + pltpu.roll(real, 64, 1)], axis=0
    )
    w1, w2, w3 = split3(weight)
    wide = jnp.concatenate([w1, w2, w3], axis=1).astype(jnp.bfloat16)
    left8 = lax.broadcasted_iota(jnp.int32, (8, 128), 1) < 64
    sign8 = jnp.where(left8, 1.0, -1.0)
    row8 = lax.broadcasted_iota(jnp.int32, (8, 128), 0)

    def image(v):
        v1, v2, v3 = split3(v)
        stack = jnp.concatenate([v1, v2, v3, jnp.zeros_like(v3)], axis=0).astype(jnp.bfloat16)
        out = jnp.dot(stack, wide, preferred_element_type=jnp.float32)
        small = out[:8, 256:] + out[8:16, 128:256] + out[16:24, :128]
        return (small + (out[:8, 128:256] + out[8:16, :128])) + out[:8, :128]

    def total(x):
        return jnp.sum(x, axis=1, keepdims=True)

    def scaled(y, norms):
        inverse = lax.rsqrt(norms)
        inverse = inverse * (1.5 - 0.5 * norms * inverse * inverse)
        return y * inverse

    def line(t, j):
        return jnp.broadcast_to(t[j : j + 1], (8, 128))

    def inner(t, u):
        return jnp.broadcast_to(total(t * u), (8, 128))

    def direct(v):
        y = image(v)
        x = pltpu.roll(y, 64, 1) * sign8
        norms = jnp.zeros((8, 128), jnp.float32)
        for j in range(NM):
            yj = line(y, j)
            c_real = inner(yj, y)
            norm = line(c_real, j) + 1e-06
            norms = jnp.where(row8 == j, norm, norms)
            if j + 1 < NM:
                xj = line(x, j)
                c_imag = inner(yj, x)
                scale = jnp.where(row8 > j, 1.0 / norm, 0.0)
                a, b = c_real * scale, c_imag * scale
                y, x = y - (a * yj - b * xj), x - (a * xj + b * yj)
        return scaled(y, norms)

    def sweep(index, v):
        y = image(v)
        x = pltpu.roll(y, 64, 1) * sign8
        norms = jnp.zeros((8, 128), jnp.float32)
        g_real = [inner(line(y, j), y) for j in range(NM)]
        g_imag = [inner(line(y, j), x) for j in range(NM - 1)]
        for j in range(NM):
            square_j = jnp.maximum(line(g_real[j], j), 0.0)
            norm = square_j + 1e-06
            norms = jnp.where(row8 == j, norm, norms)
            if j + 1 < NM:
                yj, xj = line(y, j), line(x, j)
                inverse = 1.0 / norm
                scale = jnp.where(row8 > j, inverse, 0.0)
                a, b = g_real[j] * scale, g_imag[j] * scale
                y, x = y - (a * yj - b * xj), x - (a * xj + b * yj)
                both = inverse * (2.0 - square_j * inverse)
                e_real, e_imag = g_real[j] * both, g_imag[j] * both
                for k in range(j + 1, NM):
                    c_real, c_imag = line(g_real[j], k), line(g_imag[j], k)
                    g_real[k] = g_real[k] - (c_real * e_real + c_imag * e_imag)
                    if k + 1 < NM:
                        g_imag[k] = g_imag[k] - (c_real * e_imag - c_imag * e_real)
        return scaled(y, norms)

    basis = direct(lax.fori_loop(1, ITERS - 1, sweep, direct(start)))
    energy = total(basis * image(basis))
    coef = basis.astype(jnp.bfloat16).astype(jnp.float32)
    proj_one = proj_real - pltpu.roll(proj_imag, 64, 1)
    proj_two = proj_imag + pltpu.roll(proj_real, 64, 1)
    corr_real = total(coef * proj_one)
    corr_imag = total(coef * proj_two)
    gain = 1.0 / jnp.sqrt(energy + 1e-06)
    tilt_real = gain * corr_real
    tilt_imag = gain * corr_imag
    size = jnp.sqrt(jnp.maximum(tilt_real * tilt_real + tilt_imag * tilt_imag, 0.25))
    factor_real = gain * tilt_real / size
    factor_imag = -gain * tilt_imag / size
    lane8 = lax.broadcasted_iota(jnp.int32, (8, 128), 1)
    facts = jnp.zeros((8, 128), jnp.float32)
    for i, value in enumerate((factor_real, factor_imag, energy)):
        for j, piece in enumerate(split3(jnp.broadcast_to(value, (8, 128)))):
            facts = jnp.where(lane8 == 3 * j + i, piece, facts)
    return jnp.concatenate([coef, facts], axis=0).astype(jnp.bfloat16)


def project_kernel(coeff_ref, share_ref, weight_ref, out_ref, energy_ref):
    inverse = 1.0 / jnp.sqrt(weight_ref[...])
    lane = lax.broadcasted_iota(jnp.int32, (8, 128), 1)
    sign = jnp.where(lane < 64, 1.0, -1.0)
    place = lax.broadcasted_iota(jnp.int32, (8, NF), 1)
    step = out_ref.shape[0]
    first = pl.program_id(0) * step
    energies = energy_ref[...]
    for i in range(step):
        tile = share_ref[first + i].astype(jnp.float32)
        coef, parts = tile[:8], tile[8:]
        facts = parts + pltpu.roll(parts, 125, 1) + pltpu.roll(parts, 122, 1)
        rows16 = jnp.concatenate([coef * sign, pltpu.roll(coef, 64, 1)], axis=0)
        image = jnp.dot(
            rows16.astype(jnp.bfloat16), coeff_ref[first + i], preferred_element_type=jnp.float32
        )
        real, imag = image[:8], image[8:]
        turn_real, turn_imag = facts[:, 0:1], facts[:, 1:2]
        out_ref[i, :8] = (real * turn_real - imag * turn_imag) * inverse
        out_ref[i, 8:] = (real * turn_imag + imag * turn_real) * inverse
        energies = jnp.where(place == first + i, facts[:, 2:3], energies)
    energy_ref[...] = energies


def project(coeffs, shares, weights):
    lanes = coeffs.shape[2]
    step = 8
    vmem = pl.BlockSpec(memory_space=pltpu.VMEM)
    return pl.pallas_call(
        project_kernel,
        grid=(NF // step,),
        out_shape=(
            jax.ShapeDtypeStruct((NF, 2 * NM, lanes), jnp.float32),
            jax.ShapeDtypeStruct((NM, NF), jnp.float32),
        ),
        in_specs=[vmem, vmem, pl.BlockSpec((1, lanes), lambda i: (0, 0))],
        out_specs=(
            pl.BlockSpec((step, 16, lanes), lambda i: (i, 0, 0)),
            pl.BlockSpec((NM, NF), lambda i: (0, 0)),
        ),
        compiler_params=pltpu.CompilerParams(vmem_limit_bytes=6 << 20),
        name="project",
    )(coeffs, shares, weights)


def shards(snapshots, weights, reference_field, start_basis):
    axes = ("grp", "row")
    devices, inner = lax.axis_size(axes), lax.axis_size("row")
    total_rows = snapshots.shape[1] * devices
    start = jnp.transpose(start_basis, (1, 2, 3, 0))
    coeffs, shares = transform(
        total_rows, devices, inner,
        snapshots, jnp.asarray(pair_tables()), weights[None], reference_field[None], start,
    )
    modes, energies = project(coeffs, shares, weights[None])
    return modes, energies.T


def solution(mesh):
    in_specs = (P(None, ("grp", "row")), P(("grp", "row")), P(("grp", "row")), P())
    out_specs = (P(None, None, ("grp", "row")), P())
    return jax.shard_map(shards, mesh=mesh, in_specs=in_specs, out_specs=out_specs, check_vma=False)
```

```python
import functools
import math

import numpy as np
import jax
import jax.numpy as jnp
from jax import lax
from jax.experimental import pallas as pl
from jax.experimental.pallas import tpu as pltpu
from jax.sharding import PartitionSpec as P

NFFT = 256
NBLK = 63
NF = 64
NM = 8
ITERS = 12
XC = 256
MESH = pl.DeviceIdType.MESH


def dft_table():
    steps = np.arange(NFFT, dtype=np.int32)
    bins = np.arange(1, NF + 1, dtype=np.int32)
    wrapped = bins[:, None] * steps[None, :] % NFFT
    angles = np.float32(2.0 * math.pi / NFFT) * wrapped.astype(np.float32)
    taper = np.float32(0.5) - np.float32(0.5) * np.cos(
        np.float32(2.0 * math.pi / NFFT) * steps.astype(np.float32)
    )
    scaled = taper / np.sqrt(np.sum(taper * taper))
    stacked = np.stack([np.cos(angles), -np.sin(angles)]) * scaled[None, None, :]
    return stacked.astype(jnp.bfloat16)


def pair_tables():
    rows = dft_table().reshape(2 * NF, NFFT)
    tables = np.zeros((8, 256, 384), rows.dtype)
    for r in range(8):
        for g in range(16):
            for w in range(8):
                source = rows[8 * g + (w - r) % 8]
                tables[r, 16 * g + 2 * w, :256] = source
                tables[r, 16 * g + 2 * w + 1, 128:] = source
    return tables


def packed_masks():
    row = lax.broadcasted_iota(jnp.int32, (64, 128), 0)
    lane = lax.broadcasted_iota(jnp.int32, (64, 128), 1)
    left = lane < 64
    return left, jnp.where(left, 1.0, -1.0), row <= lane % 64


def transform_kernel(
    total_rows, devices, inner,
    snap_ref, table_hbm, weight_hbm, field_hbm, start_hbm,
    modes_ref, energy_ref,
    coeff_ref, share_ref, buf, stage_a, stage_b, full_a, full_b, table_ref, weight_ref, field_ref, start_ref, gram_ref, pair_slots, slots,
    snap_sems, side_sems, pair_sems, sum_send, sum_recv, share_send, share_recv,
):
    pieces = 4
    piece_rows = snap_ref.shape[0] // pieces
    chunks = snap_ref.shape[1] // XC
    rows = snap_ref.shape[0]
    chips = devices // 2
    grp, row = lax.axis_index("grp"), lax.axis_index("row")
    me = grp * inner + row
    mine = lax.div(me, 2)
    core = lax.rem(me, 2)
    is_owner = core == lax.rem(mine, 2)

    def device(index):
        return (lax.div(index, inner), lax.rem(index, inner))

    barrier = pltpu.get_barrier_semaphore()

    side_y = lax.rem(lax.div(row, 2), 4)
    side_z = lax.div(row, 8)
    xs = [lax.rem(grp + d, 4) for d in range(4)]
    ys = [lax.rem(side_y + d, 4) for d in range(4)]
    zs = [lax.rem(side_z + d, 4) for d in range(4)]
    rows_of = {
        (z, y, c): zs[z] * 8 + ys[y] * 2 + (1 - core if c else core)
        for z in range(4) for y in range(4) for c in range(2)
    }

    def greet(there, key):
        pl.semaphore_signal(barrier, inc=1, device_id=(there, rows_of[key]), device_id_type=MESH)

    def piece_copy(chunk, slot, piece):
        lanes = pl.ds(pl.multiple_of(chunk * XC, XC), XC)
        span = pl.ds(piece * piece_rows, piece_rows)
        return pltpu.make_async_copy(
            snap_ref.at[span, lanes], buf.at[slot, span, :], snap_sems.at[slot, piece]
        )

    side = [
        pltpu.make_async_copy(source, target, side_sems.at[i])
        for i, (source, target) in enumerate((
            (weight_hbm, weight_ref), (field_hbm, field_ref), (table_hbm, table_ref), (start_hbm, start_ref),
        ))
    ]
    for i in (0, 1, 2):
        side[i].start()
    for piece in range(pieces):
        piece_copy(0, 0, piece).start()
    side[3].start()
    for slot in range(2):
        buf[slot, rows:, :] = jnp.zeros((128, XC), jnp.bfloat16)
    word = lax.broadcasted_iota(jnp.int32, (16, XC), 0) // 2
    row256 = lax.broadcasted_iota(jnp.int32, (256, XC), 0)
    is_odd = row256 % 2 == 1
    real_half = row256 < 128
    bits = [(word // s) % 2 == 1 for s in (1, 2, 4)]
    stages = (stage_a, stage_b)
    for i in (0, 1, 2):
        side[i].wait()

    def network(source, g, group, lanes):
        tiles = [source[r, 16 * g : 16 * g + 16, :] for r in range(8)]
        for level, bit in zip((1, 2, 4), bits):
            tiles = [jnp.where(bit, tiles[(m + level) % 8], tiles[m]) for m in range(8)]
        part, base = g // 8, 8 * (g % 8)
        for i in range(8):
            first = part * 64 + group * 16
            coeff_ref[base + i, first : first + 16, lanes] = tiles[(-i) % 8]

    def chunk_step(chunk, carry):
        first_chunk = isinstance(chunk, int)
        if first_chunk:
            slot, lanes, before = 0, slice(0, XC), None
            for piece in range(pieces):
                piece_copy(1, 1, piece).start()
            piece_copy(0, 0, 0).wait()
        else:
            slot = lax.rem(chunk, 2)
            lanes = pl.ds(pl.multiple_of(chunk * XC, XC), XC)
            before = pl.ds(pl.multiple_of((chunk - 1) * XC, XC), XC)

            @pl.when(chunk + 1 < chunks)
            def _():
                for piece in range(pieces):
                    piece_copy(chunk + 1, 1 - slot, piece).start()

            for piece in range(pieces):
                piece_copy(chunk, slot, piece).wait()

        root = jnp.sqrt(weight_ref[:, lanes])
        for group in range(4):
            if first_chunk and group < 3:
                piece_copy(0, 0, group + 1).wait()
            target, source = stages[group % 2], stages[(group + 1) % 2]
            for r in range(8):
                first = (group * 8 + r) * 256
                out = jnp.dot(
                    table_ref[r], buf[slot, first : first + 384, :], preferred_element_type=jnp.float32
                )
                out = out * root
                if r == 7 and group == 3:
                    probe = jnp.where(real_half, root * field_ref[:, lanes], 0.0)
                    out = jnp.where(is_odd, probe, out)
                target[r] = out.astype(jnp.bfloat16)
                for g in (2 * r, 2 * r + 1) if group or not first_chunk else ():
                    network(source, g, (group + 3) % 4, before if group == 0 else lanes)
        there = grp if first_chunk else lax.rem(grp + chunk, 4)
        for key in rows_of:
            if not (first_chunk and key == (0, 0, 0)):
                greet(there, key)
        return carry

    chunk_step(0, 0)
    lax.fori_loop(1, chunks, chunk_step, 0)
    for g in range(16):
        network(stages[1], g, 3, slice((chunks - 1) * XC, chunks * XC))
    pl.semaphore_wait(barrier, devices - 1)
    left, sign, upper = packed_masks()

    def owner(parity, i, u):
        far = (2, 3, 1, 0)
        turn = lax.rem(parity + side_y, 2) + 2 * (1 - u % 2)
        return xs[far[i]] * 16 + zs[far[u // 2]] * 4 + lax.rem(side_y + turn, 4)

    def gram(f):
        block = coeff_ref[f]
        return lax.dot_general(
            block, block, (((1,), (1,)), ((), ())), preferred_element_type=jnp.float32
        )

    def pack(full):
        packed = full[:64] + pltpu.roll(full[64:], 64, 1) * sign
        turned = pltpu.roll(packed, 64, 1)
        top = jnp.where(upper, packed, turned)
        bottom = jnp.where(upper, turned, packed)
        return jnp.where(left[:32], top[:32], bottom[32:])

    def pair_give(f):
        return pltpu.make_async_remote_copy(
            src_ref=gram_ref.at[f],
            dst_ref=pair_slots.at[lax.div(f, 2)],
            send_sem=sum_send,
            recv_sem=pair_sems.at[lax.div(f, 2)],
            device_id=device(me + 1 - 2 * core),
            device_id_type=MESH,
        )

    def give(f):
        return pltpu.make_async_remote_copy(
            src_ref=gram_ref.at[f],
            dst_ref=slots.at[mine],
            send_sem=sum_send,
            recv_sem=sum_recv,
            device_id=device(2 * f + core),
            device_id_type=MESH,
        )

    order = ((0, 0), (0, 1), (1, 0), (0, 2), (1, 1), (0, 3), (1, 2), (1, 3))
    batches = [
        (own, [owner(core if own else 1 - core, i, u) for u in range(8)]) for own, i in order
    ]
    fulls = (full_a, full_b)
    last = len(batches) - 1
    for t in range(len(batches) + 1):
        if t > 0 and batches[t - 1][0]:
            for f in batches[t - 1][1]:
                half = pair_slots.at[lax.div(f, 2)]
                pltpu.make_async_copy(half, half, pair_sems.at[lax.div(f, 2)]).wait()
        if t > 1:
            for f in batches[t - 2][1]:
                (give if batches[t - 2][0] else pair_give)(f).start()
        for u in range(8):
            if t <= last:
                fulls[t % 2][u] = gram(batches[t][1][u])
            if t > 0:
                own, fs = batches[t - 1]
                packed = pack(fulls[(t - 1) % 2][u])
                if own:
                    packed = packed + pair_slots[lax.div(fs[u], 2)]
                gram_ref[fs[u]] = packed
    for f in batches[last][1][:-1]:
        give(f).start()
    pad = 48 + 2 * lax.rem(7 + mine, 8) + 1

    def all_of(ref, count, sem):
        part = ref.at[pl.ds(0, count)]
        pltpu.make_async_copy(part, part, sem).wait()

    def tile_came(f):
        tile = share_ref.at[f]
        pltpu.make_async_copy(tile, tile, share_recv.at[f]).wait()

    def near(d):
        return min(d, 4 - d)

    def far_off(x, z, y):
        return near(x) + near(z) + near(y)

    @pl.when(jnp.logical_not(is_owner))
    def _():
        give(batches[last][1][-1]).start()
        all_of(gram_ref, NF, sum_send)
        side[3].wait()
        tile_came(mine)

    @pl.when(is_owner)
    def _():
        slots[mine] = gram_ref[mine]
        side[3].wait()
        start = start_tile(start_ref, mine)
        all_of(slots, chips - 1, sum_recv)

        def add(i, total):
            for j in range(8):
                total = total + slots[i * 8 + j]
            return total

        packed = lax.fori_loop(0, chips // 8, add, jnp.zeros((32, 128), jnp.float32))
        share_ref[mine] = solve_tile(packed, start, pad, total_rows)
        all_of(gram_ref, NF - 1, sum_send)

        peers = [(x, key) for x in range(4) for key in rows_of if (x, key) != (0, (0, 0, 0))]
        peers.sort(key=lambda p: -far_off(p[0], *p[1][:2]))
        for x, key in peers:
            pltpu.make_async_remote_copy(
                src_ref=share_ref.at[mine],
                dst_ref=share_ref.at[mine],
                send_sem=share_send,
                recv_sem=share_recv.at[mine],
                device_id=(xs[x], rows_of[key]),
                device_id_type=MESH,
            ).start()

    inverse_root = 1.0 / jnp.sqrt(weight_ref[...])
    lane8 = lax.broadcasted_iota(jnp.int32, (8, 128), 1)
    sign8 = jnp.where(lane8 < 64, 1.0, -1.0)
    place = lax.broadcasted_iota(jnp.int32, (NM, NF), 1)
    steps = [(x, z, y) for x in range(4) for z in range(4) for y in range(4)]
    steps.sort(key=lambda p: far_off(*p))
    energies = jnp.zeros((NM, NF), jnp.float32)
    bounds = (0, 22, 42, 57, 64)
    for low, high in zip(bounds[:-1], bounds[1:]):
        fs = [xs[x] * 16 + zs[z] * 4 + ys[y] for x, z, y in steps[low:high]]
        for f in fs[1:] if low == 0 else fs:
            tile_came(f)
        for f in fs:
            tile = share_ref[f].astype(jnp.float32)
            coef, parts = tile[:8], tile[8:]
            facts = parts + pltpu.roll(parts, 125, 1) + pltpu.roll(parts, 122, 1)
            rows16 = jnp.concatenate([coef * sign8, pltpu.roll(coef, 64, 1)], axis=0)
            image = jnp.dot(
                rows16.astype(jnp.bfloat16), coeff_ref[f], preferred_element_type=jnp.float32
            )
            real, imag = image[:8], image[8:]
            turn_real, turn_imag = facts[:, 0:1], facts[:, 1:2]
            modes_ref[f, :8] = (real * turn_real - imag * turn_imag) * inverse_root
            modes_ref[f, 8:] = (real * turn_imag + imag * turn_real) * inverse_root
            energies = jnp.where(place == f, facts[:, 2:3], energies)
    energy_ref[...] = energies

    @pl.when(is_owner)
    def _():
        for count in (NF, devices - 1 - NF):
            all_of(share_ref, count, share_send)


def start_tile(start_ref, mine):
    lane = lax.broadcasted_iota(jnp.int32, (8, 128), 1)
    ours = lax.broadcasted_iota(jnp.int32, (8, NF), 1) == mine
    tile = jnp.zeros((8, 128), jnp.float32)

    def some(i, tile):
        for j in range(21):
            b = i * 21 + j
            word, e = lax.div(b, 2), lax.rem(b, 2)
            place = 16 * lax.div(word, 8) + 2 * lax.rem(lax.rem(word, 8) + mine, 8) + e
            for p in range(2):
                column = jnp.sum(jnp.where(ours, start_ref[p, b], 0.0), axis=1, keepdims=True)
                tile = jnp.where(lane == 64 * p + place, column, tile)
        return tile

    return lax.fori_loop(0, NBLK // 21, some, tile)


def transform(total_rows, devices, inner, snapshots, tables, weights, field, start):
    rows, lanes = snapshots.shape
    vmem = pl.BlockSpec(memory_space=pltpu.VMEM)
    return pl.pallas_call(
        functools.partial(transform_kernel, total_rows, devices, inner),
        out_shape=(
            pltpu.VMEM((NF, 2 * NM, lanes), jnp.float32),
            pltpu.VMEM((NM, NF), jnp.float32),
        ),
        in_specs=[pl.BlockSpec(memory_space=pltpu.HBM)] * 5,
        out_specs=(vmem, vmem),
        scratch_shapes=[
            pltpu.VMEM((NF, 128, lanes), jnp.bfloat16),
            pltpu.VMEM((NF, 16, 128), jnp.bfloat16),
            pltpu.VMEM((2, rows + 128, XC), jnp.bfloat16),
            pltpu.VMEM((8, 256, XC), jnp.bfloat16),
            pltpu.VMEM((8, 256, XC), jnp.bfloat16),
            pltpu.VMEM((8, 128, 128), jnp.float32),
            pltpu.VMEM((8, 128, 128), jnp.float32),
            pltpu.VMEM(tables.shape, tables.dtype),
            pltpu.VMEM(weights.shape, weights.dtype),
            pltpu.VMEM(field.shape, field.dtype),
            pltpu.VMEM(start.shape, start.dtype),
            pltpu.VMEM((NF, 32, 128), jnp.float32),
            pltpu.VMEM((NF // 2, 32, 128), jnp.float32),
            pltpu.VMEM((devices // 2, 32, 128), jnp.float32),
            pltpu.SemaphoreType.DMA((2, 4)),
            pltpu.SemaphoreType.DMA((4,)),
            pltpu.SemaphoreType.DMA((NF // 2,)),
            pltpu.SemaphoreType.DMA,
            pltpu.SemaphoreType.DMA,
            pltpu.SemaphoreType.DMA,
            pltpu.SemaphoreType.DMA((NF,)),
        ],
        compiler_params=pltpu.CompilerParams(
            vmem_limit_bytes=61200 * 1024, collective_id=0, has_side_effects=True
        ),
        name="transform",
    )(snapshots, tables, weights, field, start)


def split3(x):
    first = x.astype(jnp.bfloat16).astype(jnp.float32)
    rest = x - first
    second = rest.astype(jnp.bfloat16).astype(jnp.float32)
    return first, second, rest - second


def solve_tile(packed, start, pad, total_rows):
    row = lax.broadcasted_iota(jnp.int32, (64, 128), 0)
    lane = lax.broadcasted_iota(jnp.int32, (64, 128), 1)
    left = lane < 64
    stacked = jnp.concatenate([packed, pltpu.roll(packed, 64, 1)], axis=0)
    stacked = jnp.where(left, stacked, 0.0)
    square = jnp.concatenate([stacked, jnp.zeros_like(stacked)], axis=0)
    flipped = jnp.transpose(square)[:64]
    real = jnp.where(row <= lane, stacked, flipped)
    imag = jnp.where(row > lane, stacked, jnp.where(row < lane, -flipped, 0.0))
    real = jnp.where(left, real, 0.0)
    imag = jnp.where(left, imag, 0.0)
    at_pad = row == pad
    root_total = 1.0 / math.sqrt(total_rows)
    proj_real = jnp.sum(jnp.where(at_pad, real, 0.0), axis=0, keepdims=True) * root_total
    proj_imag = jnp.sum(jnp.where(at_pad, imag, 0.0), axis=0, keepdims=True) * root_total
    inside = jnp.logical_and(jnp.logical_not(at_pad), lane != pad)
    inside_line = lax.broadcasted_iota(jnp.int32, (1, 128), 1) != pad
    proj_real = jnp.where(inside_line, proj_real, 0.0)
    proj_imag = jnp.where(inside_line, proj_imag, 0.0)
    real = jnp.where(inside, real, 0.0) * (1.0 / total_rows)
    imag = jnp.where(inside, imag, 0.0) * (1.0 / total_rows)
    weight = jnp.concatenate(
        [real - pltpu.roll(imag, 64, 1), imag + pltpu.roll(real, 64, 1)], axis=0
    )
    w1, w2, w3 = split3(weight)
    wide = jnp.concatenate([w1, w2, w3], axis=1).astype(jnp.bfloat16)
    left8 = lax.broadcasted_iota(jnp.int32, (8, 128), 1) < 64
    sign8 = jnp.where(left8, 1.0, -1.0)
    row8 = lax.broadcasted_iota(jnp.int32, (8, 128), 0)

    def image(v):
        v1, v2, v3 = split3(v)
        stack = jnp.concatenate([v1, v2, v3, jnp.zeros_like(v3)], axis=0).astype(jnp.bfloat16)
        out = jnp.dot(stack, wide, preferred_element_type=jnp.float32)
        small = out[:8, 256:] + out[8:16, 128:256] + out[16:24, :128]
        return (small + (out[:8, 128:256] + out[8:16, :128])) + out[:8, :128]

    def total(x):
        return jnp.sum(x, axis=1, keepdims=True)

    def scaled(y, norms):
        inverse = lax.rsqrt(norms)
        inverse = inverse * (1.5 - 0.5 * norms * inverse * inverse)
        return y * inverse

    def line(t, j):
        return jnp.broadcast_to(t[j : j + 1], (8, 128))

    def inner(t, u):
        return jnp.broadcast_to(total(t * u), (8, 128))

    def direct(v):
        y = image(v)
        x = pltpu.roll(y, 64, 1) * sign8
        norms = jnp.zeros((8, 128), jnp.float32)
        for j in range(NM):
            yj = line(y, j)
            c_real = inner(yj, y)
            norm = line(c_real, j) + 1e-06
            norms = jnp.where(row8 == j, norm, norms)
            if j + 1 < NM:
                xj = line(x, j)
                c_imag = inner(yj, x)
                scale = jnp.where(row8 > j, 1.0 / norm, 0.0)
                a, b = c_real * scale, c_imag * scale
                y, x = y - (a * yj - b * xj), x - (a * xj + b * yj)
        return scaled(y, norms)

    def sweep(index, v):
        y = image(v)
        x = pltpu.roll(y, 64, 1) * sign8
        norms = jnp.zeros((8, 128), jnp.float32)
        g_real = [inner(line(y, j), y) for j in range(NM)]
        g_imag = [inner(line(y, j), x) for j in range(NM - 1)]
        for j in range(NM):
            square_j = jnp.maximum(line(g_real[j], j), 0.0)
            norm = square_j + 1e-06
            norms = jnp.where(row8 == j, norm, norms)
            if j + 1 < NM:
                yj, xj = line(y, j), line(x, j)
                inverse = 1.0 / norm
                scale = jnp.where(row8 > j, inverse, 0.0)
                a, b = g_real[j] * scale, g_imag[j] * scale
                y, x = y - (a * yj - b * xj), x - (a * xj + b * yj)
                both = inverse * (2.0 - square_j * inverse)
                e_real, e_imag = g_real[j] * both, g_imag[j] * both
                for k in range(j + 1, NM):
                    c_real, c_imag = line(g_real[j], k), line(g_imag[j], k)
                    g_real[k] = g_real[k] - (c_real * e_real + c_imag * e_imag)
                    if k + 1 < NM:
                        g_imag[k] = g_imag[k] - (c_real * e_imag - c_imag * e_real)
        return scaled(y, norms)

    basis = direct(lax.fori_loop(1, ITERS - 1, sweep, direct(start)))
    energy = total(basis * image(basis))
    coef = basis.astype(jnp.bfloat16).astype(jnp.float32)
    proj_one = proj_real - pltpu.roll(proj_imag, 64, 1)
    proj_two = proj_imag + pltpu.roll(proj_real, 64, 1)
    corr_real = total(coef * proj_one)
    corr_imag = total(coef * proj_two)
    gain = 1.0 / jnp.sqrt(energy + 1e-06)
    tilt_real = gain * corr_real
    tilt_imag = gain * corr_imag
    size = jnp.sqrt(jnp.maximum(tilt_real * tilt_real + tilt_imag * tilt_imag, 0.25))
    factor_real = gain * tilt_real / size
    factor_imag = -gain * tilt_imag / size
    lane8 = lax.broadcasted_iota(jnp.int32, (8, 128), 1)
    facts = jnp.zeros((8, 128), jnp.float32)
    for i, value in enumerate((factor_real, factor_imag, energy)):
        for j, piece in enumerate(split3(jnp.broadcast_to(value, (8, 128)))):
            facts = jnp.where(lane8 == 3 * j + i, piece, facts)
    return jnp.concatenate([coef, facts], axis=0).astype(jnp.bfloat16)


def shards(snapshots, weights, reference_field, start_basis):
    axes = ("grp", "row")
    devices, inner = lax.axis_size(axes), lax.axis_size("row")
    total_rows = snapshots.shape[1] * devices
    start = jnp.transpose(start_basis, (1, 2, 3, 0))
    modes, energies = transform(
        total_rows, devices, inner,
        snapshots, jnp.asarray(pair_tables()), weights[None], reference_field[None], start,
    )
    return modes, energies.T


def solution(mesh):
    in_specs = (P(None, ("grp", "row")), P(("grp", "row")), P(("grp", "row")), P())
    out_specs = (P(None, None, ("grp", "row")), P())
    return jax.shard_map(shards, mesh=mesh, in_specs=in_specs, out_specs=out_specs, check_vma=False)
```

```python
import functools
import math

import numpy as np
import jax
import jax.numpy as jnp
from jax import lax
from jax.experimental import pallas as pl
from jax.experimental.pallas import tpu as pltpu
from jax.sharding import PartitionSpec as P

NFFT = 256
NBLK = 63
NF = 64
NM = 8
ITERS = 12
XC = 256
MESH = pl.DeviceIdType.MESH


def dft_table():
    steps = np.arange(NFFT, dtype=np.int32)
    bins = np.arange(1, NF + 1, dtype=np.int32)
    wrapped = bins[:, None] * steps[None, :] % NFFT
    angles = np.float32(2.0 * math.pi / NFFT) * wrapped.astype(np.float32)
    taper = np.float32(0.5) - np.float32(0.5) * np.cos(
        np.float32(2.0 * math.pi / NFFT) * steps.astype(np.float32)
    )
    scaled = taper / np.sqrt(np.sum(taper * taper))
    stacked = np.stack([np.cos(angles), -np.sin(angles)]) * scaled[None, None, :]
    return stacked.astype(jnp.bfloat16)


def pair_tables():
    rows = dft_table().reshape(2 * NF, NFFT)
    tables = np.zeros((8, 256, 384), rows.dtype)
    for r in range(8):
        for g in range(16):
            for w in range(8):
                source = rows[8 * g + (w - r) % 8]
                tables[r, 16 * g + 2 * w, :256] = source
                tables[r, 16 * g + 2 * w + 1, 128:] = source
    return tables


def packed_masks():
    row = lax.broadcasted_iota(jnp.int32, (64, 128), 0)
    lane = lax.broadcasted_iota(jnp.int32, (64, 128), 1)
    left = lane < 64
    return left, jnp.where(left, 1.0, -1.0), row <= lane % 64


def transform_kernel(
    total_rows, devices, inner,
    snap_ref, table_hbm, weight_hbm, field_hbm, start_hbm,
    coeff_ref, share_ref,
    buf, stage_a, stage_b, full_a, full_b, table_ref, weight_ref, field_ref, start_ref, gram_ref, pair_slots, slots,
    snap_sems, side_sems, pair_sems, sum_send, sum_recv, share_send, share_recv, relay_recv,
):
    pieces = 4
    piece_rows = snap_ref.shape[0] // pieces
    chunks = snap_ref.shape[1] // XC
    rows = snap_ref.shape[0]
    chips = devices // 2
    grp, row = lax.axis_index("grp"), lax.axis_index("row")
    me = grp * inner + row
    mine = lax.div(me, 2)
    core = lax.rem(me, 2)
    is_owner = core == lax.rem(mine, 2)

    def device(index):
        return (lax.div(index, inner), lax.rem(index, inner))

    barrier = pltpu.get_barrier_semaphore()

    side_y = lax.rem(lax.div(row, 2), 4)
    side_z = lax.div(row, 8)
    xs = [lax.rem(grp + d, 4) for d in range(4)]
    ys = [lax.rem(side_y + d, 4) for d in range(4)]
    zs = [lax.rem(side_z + d, 4) for d in range(4)]
    rows_of = {
        (z, y, c): zs[z] * 8 + ys[y] * 2 + (1 - core if c else core)
        for z in range(4) for y in range(4) for c in range(2)
    }

    def greet(there, key):
        pl.semaphore_signal(barrier, inc=1, device_id=(there, rows_of[key]), device_id_type=MESH)

    def piece_copy(chunk, slot, piece):
        lanes = pl.ds(pl.multiple_of(chunk * XC, XC), XC)
        span = pl.ds(piece * piece_rows, piece_rows)
        return pltpu.make_async_copy(
            snap_ref.at[span, lanes], buf.at[slot, span, :], snap_sems.at[slot, piece]
        )

    side = [
        pltpu.make_async_copy(source, target, side_sems.at[i])
        for i, (source, target) in enumerate((
            (weight_hbm, weight_ref), (field_hbm, field_ref), (table_hbm, table_ref), (start_hbm, start_ref),
        ))
    ]
    for i in (0, 1, 2):
        side[i].start()
    for piece in range(pieces):
        piece_copy(0, 0, piece).start()
    side[3].start()
    for slot in range(2):
        buf[slot, rows:, :] = jnp.zeros((128, XC), jnp.bfloat16)
    word = lax.broadcasted_iota(jnp.int32, (16, XC), 0) // 2
    row256 = lax.broadcasted_iota(jnp.int32, (256, XC), 0)
    is_odd = row256 % 2 == 1
    real_half = row256 < 128
    bits = [(word // s) % 2 == 1 for s in (1, 2, 4)]
    stages = (stage_a, stage_b)
    for i in (0, 1, 2):
        side[i].wait()

    def network(source, g, group, lanes):
        tiles = [source[r, 16 * g : 16 * g + 16, :] for r in range(8)]
        for level, bit in zip((1, 2, 4), bits):
            tiles = [jnp.where(bit, tiles[(m + level) % 8], tiles[m]) for m in range(8)]
        part, base = g // 8, 8 * (g % 8)
        for i in range(8):
            first = part * 64 + group * 16
            coeff_ref[base + i, first : first + 16, lanes] = tiles[(-i) % 8]

    def chunk_step(chunk, carry):
        first_chunk = isinstance(chunk, int)
        if first_chunk:
            slot, lanes, before = 0, slice(0, XC), None
            for piece in range(pieces):
                piece_copy(1, 1, piece).start()
            piece_copy(0, 0, 0).wait()
        else:
            slot = lax.rem(chunk, 2)
            lanes = pl.ds(pl.multiple_of(chunk * XC, XC), XC)
            before = pl.ds(pl.multiple_of((chunk - 1) * XC, XC), XC)

            @pl.when(chunk + 1 < chunks)
            def _():
                for piece in range(pieces):
                    piece_copy(chunk + 1, 1 - slot, piece).start()

            for piece in range(pieces):
                piece_copy(chunk, slot, piece).wait()

        root = jnp.sqrt(weight_ref[:, lanes])
        for group in range(4):
            if first_chunk and group < 3:
                piece_copy(0, 0, group + 1).wait()
            target, source = stages[group % 2], stages[(group + 1) % 2]
            for r in range(8):
                first = (group * 8 + r) * 256
                out = jnp.dot(
                    table_ref[r], buf[slot, first : first + 384, :], preferred_element_type=jnp.float32
                )
                out = out * root
                if r == 7 and group == 3:
                    probe = jnp.where(real_half, root * field_ref[:, lanes], 0.0)
                    out = jnp.where(is_odd, probe, out)
                target[r] = out.astype(jnp.bfloat16)
                for g in (2 * r, 2 * r + 1) if group or not first_chunk else ():
                    network(source, g, (group + 3) % 4, before if group == 0 else lanes)
        there = grp if first_chunk else lax.rem(grp + chunk, 4)
        for key in rows_of:
            if not (first_chunk and key == (0, 0, 0)):
                greet(there, key)
        return carry

    chunk_step(0, 0)
    lax.fori_loop(1, chunks, chunk_step, 0)
    for g in range(16):
        network(stages[1], g, 3, slice((chunks - 1) * XC, chunks * XC))
    pl.semaphore_wait(barrier, devices - 1)
    left, sign, upper = packed_masks()

    def owner(parity, i, u):
        far = (2, 3, 1, 0)
        turn = lax.rem(parity + side_y, 2) + 2 * (1 - u % 2)
        return xs[far[i]] * 16 + zs[far[u // 2]] * 4 + lax.rem(side_y + turn, 4)

    def gram(f):
        block = coeff_ref[f]
        return lax.dot_general(
            block, block, (((1,), (1,)), ((), ())), preferred_element_type=jnp.float32
        )

    def pack(full):
        packed = full[:64] + pltpu.roll(full[64:], 64, 1) * sign
        turned = pltpu.roll(packed, 64, 1)
        top = jnp.where(upper, packed, turned)
        bottom = jnp.where(upper, turned, packed)
        return jnp.where(left[:32], top[:32], bottom[32:])

    def pair_give(f):
        return pltpu.make_async_remote_copy(
            src_ref=gram_ref.at[f],
            dst_ref=pair_slots.at[lax.div(f, 2)],
            send_sem=sum_send,
            recv_sem=pair_sems.at[lax.div(f, 2)],
            device_id=device(me + 1 - 2 * core),
            device_id_type=MESH,
        )

    def give(f):
        return pltpu.make_async_remote_copy(
            src_ref=gram_ref.at[f],
            dst_ref=slots.at[mine],
            send_sem=sum_send,
            recv_sem=sum_recv,
            device_id=device(2 * f + core),
            device_id_type=MESH,
        )

    order = ((0, 0), (0, 1), (1, 0), (0, 2), (1, 1), (0, 3), (1, 2), (1, 3))
    batches = [
        (own, [owner(core if own else 1 - core, i, u) for u in range(8)]) for own, i in order
    ]
    fulls = (full_a, full_b)
    last = len(batches) - 1
    for t in range(len(batches) + 1):
        if t > 0 and batches[t - 1][0]:
            for f in batches[t - 1][1]:
                half = pair_slots.at[lax.div(f, 2)]
                pltpu.make_async_copy(half, half, pair_sems.at[lax.div(f, 2)]).wait()
        if t > 1:
            for f in batches[t - 2][1]:
                (give if batches[t - 2][0] else pair_give)(f).start()
        for u in range(8):
            if t <= last:
                fulls[t % 2][u] = gram(batches[t][1][u])
            if t > 0:
                own, fs = batches[t - 1]
                packed = pack(fulls[(t - 1) % 2][u])
                if own:
                    packed = packed + pair_slots[lax.div(fs[u], 2)]
                gram_ref[fs[u]] = packed
    for f in batches[last][1][:-1]:
        give(f).start()
    pad = 48 + 2 * lax.rem(7 + mine, 8) + 1

    def all_of(ref, count, sem):
        part = ref.at[pl.ds(0, count)]
        pltpu.make_async_copy(part, part, sem).wait()

    def near(d):
        return min(d, 4 - d)

    peers = [(x, z, y) for x in range(4) for z in range(4) for y in range(4)][1:]
    peers.sort(key=lambda p: -(near(p[0]) + near(p[1]) + near(p[2])))

    def share(x, key, arrival):
        pltpu.make_async_remote_copy(
            src_ref=share_ref.at[mine],
            dst_ref=share_ref.at[mine],
            send_sem=share_send,
            recv_sem=arrival,
            device_id=(xs[x], rows_of[key]),
            device_id_type=MESH,
        ).start()

    @pl.when(jnp.logical_not(is_owner))
    def _():
        give(batches[last][1][-1]).start()
        all_of(gram_ref, NF, sum_send)
        side[3].wait()
        all_of(share_ref, 1, relay_recv)
        for x, z, y in peers:
            share(x, (z, y, 0), share_recv)
        all_of(share_ref, NF - 1, share_recv)
        all_of(share_ref, NF - 1, share_send)

    @pl.when(is_owner)
    def _():
        slots[mine] = gram_ref[mine]
        side[3].wait()
        start = start_tile(start_ref, mine)
        all_of(slots, chips - 1, sum_recv)

        def add(i, total):
            for j in range(8):
                total = total + slots[i * 8 + j]
            return total

        packed = lax.fori_loop(0, chips // 8, add, jnp.zeros((32, 128), jnp.float32))
        share_ref[mine] = solve_tile(packed, start, pad, total_rows)
        all_of(gram_ref, NF - 1, sum_send)

        share(0, (0, 0, 1), relay_recv)
        for x, z, y in peers:
            share(x, (z, y, 0), share_recv)
        all_of(share_ref, NF - 1, share_recv)
        all_of(share_ref, NF, share_send)


def start_tile(start_ref, mine):
    lane = lax.broadcasted_iota(jnp.int32, (8, 128), 1)
    ours = lax.broadcasted_iota(jnp.int32, (8, NF), 1) == mine
    tile = jnp.zeros((8, 128), jnp.float32)

    def some(i, tile):
        for j in range(21):
            b = i * 21 + j
            word, e = lax.div(b, 2), lax.rem(b, 2)
            place = 16 * lax.div(word, 8) + 2 * lax.rem(lax.rem(word, 8) + mine, 8) + e
            for p in range(2):
                column = jnp.sum(jnp.where(ours, start_ref[p, b], 0.0), axis=1, keepdims=True)
                tile = jnp.where(lane == 64 * p + place, column, tile)
        return tile

    return lax.fori_loop(0, NBLK // 21, some, tile)


def transform(total_rows, devices, inner, snapshots, tables, weights, field, start):
    rows, lanes = snapshots.shape
    vmem = pl.BlockSpec(memory_space=pltpu.VMEM)
    return pl.pallas_call(
        functools.partial(transform_kernel, total_rows, devices, inner),
        out_shape=(
            pltpu.VMEM((NF, 128, lanes), jnp.bfloat16),
            pltpu.VMEM((NF, 16, 128), jnp.bfloat16),
        ),
        in_specs=[pl.BlockSpec(memory_space=pltpu.HBM)] * 5,
        out_specs=(vmem, vmem),
        scratch_shapes=[
            pltpu.VMEM((2, rows + 128, XC), jnp.bfloat16),
            pltpu.VMEM((8, 256, XC), jnp.bfloat16),
            pltpu.VMEM((8, 256, XC), jnp.bfloat16),
            pltpu.VMEM((8, 128, 128), jnp.float32),
            pltpu.VMEM((8, 128, 128), jnp.float32),
            pltpu.VMEM(tables.shape, tables.dtype),
            pltpu.VMEM(weights.shape, weights.dtype),
            pltpu.VMEM(field.shape, field.dtype),
            pltpu.VMEM(start.shape, start.dtype),
            pltpu.VMEM((NF, 32, 128), jnp.float32),
            pltpu.VMEM((NF // 2, 32, 128), jnp.float32),
            pltpu.VMEM((devices // 2, 32, 128), jnp.float32),
            pltpu.SemaphoreType.DMA((2, 4)),
            pltpu.SemaphoreType.DMA((4,)),
            pltpu.SemaphoreType.DMA((NF // 2,)),
            pltpu.SemaphoreType.DMA,
            pltpu.SemaphoreType.DMA,
            pltpu.SemaphoreType.DMA,
            pltpu.SemaphoreType.DMA,
            pltpu.SemaphoreType.DMA,
        ],
        compiler_params=pltpu.CompilerParams(
            vmem_limit_bytes=48600 * 1024, collective_id=0, has_side_effects=True
        ),
        name="transform",
    )(snapshots, tables, weights, field, start)


def split3(x):
    first = x.astype(jnp.bfloat16).astype(jnp.float32)
    rest = x - first
    second = rest.astype(jnp.bfloat16).astype(jnp.float32)
    return first, second, rest - second


def solve_tile(packed, start, pad, total_rows):
    row = lax.broadcasted_iota(jnp.int32, (64, 128), 0)
    lane = lax.broadcasted_iota(jnp.int32, (64, 128), 1)
    left = lane < 64
    stacked = jnp.concatenate([packed, pltpu.roll(packed, 64, 1)], axis=0)
    stacked = jnp.where(left, stacked, 0.0)
    square = jnp.concatenate([stacked, jnp.zeros_like(stacked)], axis=0)
    flipped = jnp.transpose(square)[:64]
    real = jnp.where(row <= lane, stacked, flipped)
    imag = jnp.where(row > lane, stacked, jnp.where(row < lane, -flipped, 0.0))
    real = jnp.where(left, real, 0.0)
    imag = jnp.where(left, imag, 0.0)
    at_pad = row == pad
    root_total = 1.0 / math.sqrt(total_rows)
    proj_real = jnp.sum(jnp.where(at_pad, real, 0.0), axis=0, keepdims=True) * root_total
    proj_imag = jnp.sum(jnp.where(at_pad, imag, 0.0), axis=0, keepdims=True) * root_total
    inside = jnp.logical_and(jnp.logical_not(at_pad), lane != pad)
    inside_line = lax.broadcasted_iota(jnp.int32, (1, 128), 1) != pad
    proj_real = jnp.where(inside_line, proj_real, 0.0)
    proj_imag = jnp.where(inside_line, proj_imag, 0.0)
    real = jnp.where(inside, real, 0.0) * (1.0 / total_rows)
    imag = jnp.where(inside, imag, 0.0) * (1.0 / total_rows)
    weight = jnp.concatenate(
        [real - pltpu.roll(imag, 64, 1), imag + pltpu.roll(real, 64, 1)], axis=0
    )
    w1, w2, w3 = split3(weight)
    wide = jnp.concatenate([w1, w2, w3], axis=1).astype(jnp.bfloat16)
    left8 = lax.broadcasted_iota(jnp.int32, (8, 128), 1) < 64
    sign8 = jnp.where(left8, 1.0, -1.0)
    row8 = lax.broadcasted_iota(jnp.int32, (8, 128), 0)

    def image(v):
        v1, v2, v3 = split3(v)
        stack = jnp.concatenate([v1, v2, v3, jnp.zeros_like(v3)], axis=0).astype(jnp.bfloat16)
        out = jnp.dot(stack, wide, preferred_element_type=jnp.float32)
        small = out[:8, 256:] + out[8:16, 128:256] + out[16:24, :128]
        return (small + (out[:8, 128:256] + out[8:16, :128])) + out[:8, :128]

    def total(x):
        return jnp.sum(x, axis=1, keepdims=True)

    def scaled(y, norms):
        inverse = lax.rsqrt(norms)
        inverse = inverse * (1.5 - 0.5 * norms * inverse * inverse)
        return y * inverse

    def line(t, j):
        return jnp.broadcast_to(t[j : j + 1], (8, 128))

    def inner(t, u):
        return jnp.broadcast_to(total(t * u), (8, 128))

    def direct(v):
        y = image(v)
        x = pltpu.roll(y, 64, 1) * sign8
        norms = jnp.zeros((8, 128), jnp.float32)
        for j in range(NM):
            yj = line(y, j)
            c_real = inner(yj, y)
            norm = line(c_real, j) + 1e-06
            norms = jnp.where(row8 == j, norm, norms)
            if j + 1 < NM:
                xj = line(x, j)
                c_imag = inner(yj, x)
                scale = jnp.where(row8 > j, 1.0 / norm, 0.0)
                a, b = c_real * scale, c_imag * scale
                y, x = y - (a * yj - b * xj), x - (a * xj + b * yj)
        return scaled(y, norms)

    def sweep(index, v):
        y = image(v)
        x = pltpu.roll(y, 64, 1) * sign8
        norms = jnp.zeros((8, 128), jnp.float32)
        g_real = [inner(line(y, j), y) for j in range(NM)]
        g_imag = [inner(line(y, j), x) for j in range(NM - 1)]
        for j in range(NM):
            square_j = jnp.maximum(line(g_real[j], j), 0.0)
            norm = square_j + 1e-06
            norms = jnp.where(row8 == j, norm, norms)
            if j + 1 < NM:
                yj, xj = line(y, j), line(x, j)
                inverse = 1.0 / norm
                scale = jnp.where(row8 > j, inverse, 0.0)
                a, b = g_real[j] * scale, g_imag[j] * scale
                y, x = y - (a * yj - b * xj), x - (a * xj + b * yj)
                both = inverse * (2.0 - square_j * inverse)
                e_real, e_imag = g_real[j] * both, g_imag[j] * both
                for k in range(j + 1, NM):
                    c_real, c_imag = line(g_real[j], k), line(g_imag[j], k)
                    g_real[k] = g_real[k] - (c_real * e_real + c_imag * e_imag)
                    if k + 1 < NM:
                        g_imag[k] = g_imag[k] - (c_real * e_imag - c_imag * e_real)
        return scaled(y, norms)

    basis = direct(lax.fori_loop(1, ITERS - 1, sweep, direct(start)))
    energy = total(basis * image(basis))
    coef = basis.astype(jnp.bfloat16).astype(jnp.float32)
    proj_one = proj_real - pltpu.roll(proj_imag, 64, 1)
    proj_two = proj_imag + pltpu.roll(proj_real, 64, 1)
    corr_real = total(coef * proj_one)
    corr_imag = total(coef * proj_two)
    gain = 1.0 / jnp.sqrt(energy + 1e-06)
    tilt_real = gain * corr_real
    tilt_imag = gain * corr_imag
    size = jnp.sqrt(jnp.maximum(tilt_real * tilt_real + tilt_imag * tilt_imag, 0.25))
    factor_real = gain * tilt_real / size
    factor_imag = -gain * tilt_imag / size
    lane8 = lax.broadcasted_iota(jnp.int32, (8, 128), 1)
    facts = jnp.zeros((8, 128), jnp.float32)
    for i, value in enumerate((factor_real, factor_imag, energy)):
        for j, piece in enumerate(split3(jnp.broadcast_to(value, (8, 128)))):
            facts = jnp.where(lane8 == 3 * j + i, piece, facts)
    return jnp.concatenate([coef, facts], axis=0).astype(jnp.bfloat16)


def project_kernel(coeff_ref, share_ref, weight_ref, out_ref, energy_ref, modes, sems):
    inverse = 1.0 / jnp.sqrt(weight_ref[...])
    lane = lax.broadcasted_iota(jnp.int32, (8, 128), 1)
    sign = jnp.where(lane < 64, 1.0, -1.0)
    place = lax.broadcasted_iota(jnp.int32, (NM, NF), 1)
    energies = jnp.zeros((NM, NF), jnp.float32)
    copies = []
    for block in range(8):
        span = slice(block * 8, block * 8 + 8)
        for f in range(block * 8, block * 8 + 8):
            tile = share_ref[f].astype(jnp.float32)
            coef, parts = tile[:8], tile[8:]
            facts = parts + pltpu.roll(parts, 125, 1) + pltpu.roll(parts, 122, 1)
            rows16 = jnp.concatenate([coef * sign, pltpu.roll(coef, 64, 1)], axis=0)
            image = jnp.dot(
                rows16.astype(jnp.bfloat16), coeff_ref[f], preferred_element_type=jnp.float32
            )
            real, imag = image[:8], image[8:]
            turn_real, turn_imag = facts[:, 0:1], facts[:, 1:2]
            modes[f, :8] = (real * turn_real - imag * turn_imag) * inverse
            modes[f, 8:] = (real * turn_imag + imag * turn_real) * inverse
            energies = jnp.where(place == f, facts[:, 2:3], energies)
        copies.append(pltpu.make_async_copy(modes.at[span], out_ref.at[span], sems.at[block]))
        copies[-1].start()
    energy_ref[...] = energies
    for copy in copies:
        copy.wait()


def project(coeffs, shares, weights):
    lanes = coeffs.shape[2]
    vmem = pl.BlockSpec(memory_space=pltpu.VMEM)
    return pl.pallas_call(
        project_kernel,
        out_shape=(
            jax.ShapeDtypeStruct((NF, 2 * NM, lanes), jnp.float32),
            jax.ShapeDtypeStruct((NM, NF), jnp.float32),
        ),
        in_specs=[vmem, vmem, vmem],
        out_specs=(pl.BlockSpec(memory_space=pltpu.HBM), vmem),
        scratch_shapes=[
            pltpu.VMEM((NF, 2 * NM, lanes), jnp.float32),
            pltpu.SemaphoreType.DMA((8,)),
        ],
        compiler_params=pltpu.CompilerParams(vmem_limit_bytes=12 << 20),
        name="project",
    )(coeffs, shares, weights)


def shards(snapshots, weights, reference_field, start_basis):
    axes = ("grp", "row")
    devices, inner = lax.axis_size(axes), lax.axis_size("row")
    total_rows = snapshots.shape[1] * devices
    start = jnp.transpose(start_basis, (1, 2, 3, 0))
    coeffs, shares = transform(
        total_rows, devices, inner,
        snapshots, jnp.asarray(pair_tables()), weights[None], reference_field[None], start,
    )
    modes, energies = project(coeffs, shares, weights[None])
    return modes, energies.T


def solution(mesh):
    in_specs = (P(None, ("grp", "row")), P(("grp", "row")), P(("grp", "row")), P())
    out_specs = (P(None, None, ("grp", "row")), P())
    return jax.shard_map(shards, mesh=mesh, in_specs=in_specs, out_specs=out_specs, check_vma=False)
```
